256 devices in a mesh: expert: 8 (over x, core), context: 32 (over y, z).
Axes of the slice: x: 4, y: 4, z: 8, core: 2. Of those that a mesh axis runs over, the one named last changes fastest.
Arguments:
- hidden: bfloat16 [8, 4096, 2048], P('expert', 'context'), may hold values from -6 to 6
- query: bfloat16 [8, 4096, 2048], P('expert', 'context'), may hold values from -120 to 120
- keys: bfloat16 [8, 4096, 512], P('expert', 'context'), may hold values from -6 to 6
- values: bfloat16 [8, 4096, 512], P('expert', 'context'), may hold values from -6 to 6
- x_inner: bfloat16 [8, 4096, 4096], P('expert', 'context'), may hold values from -6 to 6
- z_gate: bfloat16 [8, 4096, 4096], P('expert', 'context'), may hold values from -6 to 6
- dt_raw: bfloat16 [8, 4096, 4096], P('expert', 'context'), may hold values from -5 to 5
- b_proj: float32 [8, 4096, 16], P('expert', 'context'), may hold values from -0.6 to 0.6
- c_proj: float32 [8, 4096, 16], P('expert', 'context'), may hold values from -0.6 to 0.6
- conv_weight: float32 [4, 4096], replicated, may hold values from -3 to 3
- conv_bias: float32 [4096], replicated, may hold values from -3 to 3
- dt_bias: float32 [4096], replicated, may hold values from -0.5 to 0.5
- a_rate: float32 [16, 4096], replicated, may hold values from 7.324219e-05 to 0.05
- skip_gain: float32 [4096], replicated, may hold values from 0.5 to 1.5
- mamba_vector: float32 [4096], replicated, may hold values from -0.09375 to 0.09375
- attn_vector: float32 [2048], replicated, may hold values from -0.125 to 0.125
- impact_vector: float32 [2048], replicated, may hold values from -0.125 to 0.125
- norm_gain: float32 [2048], replicated, may hold values from 0.5 to 1.5
- expert_gate: bfloat16 [16, 2048, 7168], P('expert', None, 'context'), may hold values from -0.125 to 0.125
- expert_up: bfloat16 [16, 2048, 7168], P('expert', None, 'context'), may hold values from -0.125 to 0.125
- expert_vector: float32 [16, 7168], P('expert', 'context'), may hold values from -0.0625 to 0.0625
- routes: int32 [8, 4096, 2], P('expert', 'context'), may hold values from 0 to 15, all different within a row
- route_gate: float32 [8, 4096, 2], P('expert', 'context'), may hold values from 0.1 to 0.9
- lengths: int32 [8], replicated, may hold values from 1 to 4096, 20480 in all
- term_ids: int32 [8, 4096], P('expert', 'context'), may hold values from 0 to 65535
Outputs:
- token_impacts: float32 [8, 4096], P('expert', 'context')
- term_impacts: float32 [8, 65536], P('expert', 'context')
The draws below stay inside these ranges and needn't reach their ends.
All inputs are finite; a program needn't handle non-finite values.
Results may differ from the reference program's by a relative error of at most 0.009.
Values may be sent and summed in bfloat16 or wider, within the bound.
A program may use at most 192 MiB of HBM per device.

```python
import math
import jax
import jax.numpy as jnp
import numpy as np
from jax import lax

D = 2048
H = 16
HD = 128
KVH = 4
INNER = 4096
NSTATE = 16
KCONV = 4
FF = 7168
TOP = 2
VOCAB = 65536
TOK_DEV = 128
CAP = 10
SEQ = 4096
NDOCS = 8
EXPERTS = 16
N_CONTEXT = 32


def draw_query(key, part):
    drawn = jax.random.normal(key, (NDOCS, SEQ, H * HD), jnp.float32)
    return jnp.clip(drawn, -120.0, 120.0).astype(jnp.bfloat16)


def draw_dt_raw(key, part):
    block_count = SEQ // TOK_DEV
    base = jnp.clip(0.5 * jax.random.normal(jax.random.fold_in(key, 11), (NDOCS, SEQ, INNER), jnp.float32), -3.0, 3.0)
    offset = jax.random.uniform(jax.random.fold_in(key, 13), (NDOCS, block_count, 1, INNER), jnp.float32, -2.0, 1.5)
    offset = jnp.broadcast_to(offset, (NDOCS, block_count, TOK_DEV, INNER)).reshape(NDOCS, SEQ, INNER)
    return jnp.clip(base + offset, -5.0, 5.0).astype(jnp.bfloat16)


def touch_ends(entries, rng, smallest, largest):
    longest = entries.shape.index(max(entries.shape))
    spots = []
    for shift in (0, 1):
        where = [jax.random.randint(jax.random.fold_in(rng, axis), (), 0, length) for axis, length in enumerate(entries.shape)]
        where[longest] = (where[longest] + shift) % entries.shape[longest]
        spots.append(tuple(where))
    return entries.at[spots[0]].set(smallest).at[spots[1]].set(largest)


def level_of(own_key, extent, shards, smallest, largest):
    def one(axis_at, blocks):
        draws = jax.random.uniform(jax.random.fold_in(jax.random.fold_in(own_key, 6), axis_at), (blocks,), jnp.float32, smallest / len(shards), largest / len(shards))
        return jnp.repeat(jnp.exp(draws), extent[axis_at] // blocks).reshape((-1,) + (1,) * (len(extent) - axis_at - 1))

    factor_of = one(*shards[0])
    for cut in shards[1:]:
        factor_of = factor_of * one(*cut)
    return factor_of


def rank_bounds(amount, lean):
    weights = [(1 << 20) // math.isqrt(standing ** lean) + 1 for standing in range(1, amount + 1)]
    width = 1 + sum(weights) // (1 << 30)
    return np.cumsum(np.array([max(1, weight // width) for weight in weights]))


def ranked_ids(own_key, shape, number_of, lean):
    listing = rank_bounds(number_of, lean)
    pick = jax.random.randint(jax.random.fold_in(own_key, 1), shape, 0, int(listing[number_of - 1]))
    standing = jnp.searchsorted(jnp.asarray(listing, jnp.int32), pick, side="right")
    return jax.random.permutation(jax.random.fold_in(own_key, 2), number_of)[standing].astype(jnp.int32)


def different_ones(own_key, rows, count, top, lift):
    sequence = jax.random.permutation(jax.random.fold_in(own_key, 1), count)
    pull = sequence
    for power in range(3):
        pull = pull * pull // count
    pull = pull * lift // count
    chance = jax.random.randint(jax.random.fold_in(own_key, 2), (rows, count), 0, 4096) + pull
    sure = jax.random.permutation(jax.random.fold_in(own_key, 3), rows)[jnp.arange(count) % rows]
    chance = jnp.where(jnp.arange(rows)[:, None] == sure[None, :], 1 << 14, chance)
    merit = chance * count + jnp.arange(count)
    return lax.top_k(merit.astype(jnp.int32), top)[1].astype(jnp.int32)


def profile(amount, total, limit, skew):
    loads = [(1 << 20) // math.isqrt(grade ** skew) + 1 for grade in range(2, amount + 1)]
    spare, counts = total - limit - (amount - 1), [1] * (amount - 1)
    while spare > 0:
        movable = [i for i in range(amount - 1) if counts[i] < limit]
        mass, budget = sum([loads[i] for i in movable]), spare
        for i in movable:
            more = min(limit - counts[i], max(1, budget * loads[i] // mass), spare)
            counts[i] = counts[i] + more
            spare = spare - more
    return np.array([limit] + counts)


def uneven_parts(rng, count, total, limit, skew):
    if count == 2:
        one = jax.random.randint(rng, (), max(1, total - limit), min(limit, total - 1) + 1)
        return jnp.stack([one, total - one])
    sizes = jnp.asarray(profile(count, total, limit, skew), jnp.int32)
    pairs = (count - 1) // 2
    source_of, receiver = sizes[1:1 + 2 * pairs:2], sizes[2:2 + 2 * pairs:2]
    margin = jnp.minimum(source_of - 1, limit - receiver)
    shifted = jax.random.randint(jax.random.fold_in(rng, 1), (pairs,), 0, 1 << 20) % (margin + 1)
    sizes = sizes.at[1:1 + 2 * pairs:2].set(source_of - shifted).at[2:2 + 2 * pairs:2].set(receiver + shifted)
    return sizes[jax.random.permutation(jax.random.fold_in(rng, 2), count)]


def centred(stream_key, dims, spread, most, pieces=(), held_as=jnp.bfloat16):
    entries = spread * jax.random.normal(stream_key, dims, jnp.float32)
    if pieces:
        entries = entries * level_of(stream_key, dims, pieces, -0.22, 0.18)
    return jnp.clip(entries, -most, most).astype(held_as)


def setup_inputs(seed: int = 0) -> dict:
    arg_keys = jax.random.split(jax.random.key(seed), 26)
    hidden = centred(arg_keys[0], (NDOCS, SEQ, D), 1.0, 6.0, ((0, 8), (1, 32)))
    query = draw_query(jax.random.fold_in(arg_keys[25], 71), 0)
    keys = centred(arg_keys[2], (NDOCS, SEQ, KVH * HD), 1.0, 6.0, ((0, 8), (1, 32)))
    values = centred(arg_keys[3], (NDOCS, SEQ, KVH * HD), 1.0, 6.0, ((0, 8), (1, 32)))
    x_inner = centred(arg_keys[4], (NDOCS, SEQ, INNER), 1.0, 6.0, ((0, 8), (1, 32)))
    z_gate = centred(arg_keys[5], (NDOCS, SEQ, INNER), 1.0, 6.0, ((0, 8), (1, 32)))
    dt_raw = draw_dt_raw(jax.random.fold_in(arg_keys[25], 71), 0)
    b_proj = centred(arg_keys[7], (NDOCS, SEQ, NSTATE), 0.1, 0.6, ((0, 8), (1, 32)), jnp.float32)
    c_proj = centred(arg_keys[8], (NDOCS, SEQ, NSTATE), 0.1, 0.6, ((0, 8), (1, 32)), jnp.float32)
    conv_weight = centred(arg_keys[9], (KCONV, INNER), 0.5, 3.0, (), jnp.float32)
    conv_bias = centred(arg_keys[10], (INNER,), 0.5, 3.0, (), jnp.float32)
    dt_bias = jnp.clip(jax.random.uniform(arg_keys[11], (INNER,), jnp.float32, -0.5, 0.5), -0.5, 0.5)
    a_rate = jnp.clip(jnp.exp(jax.random.uniform(arg_keys[12], (NSTATE, INNER), jnp.float32, math.log(7.324219041038305e-05), math.log(0.05))), 7.324219041038305e-05, 0.05)
    skip_gain = jnp.clip(jax.random.uniform(arg_keys[13], (INNER,), jnp.float32, 0.5, 1.5), 0.5, 1.5)
    mamba_vector = centred(arg_keys[14], (INNER,), INNER ** -0.5, 0.09375, (), jnp.float32)
    attn_vector = centred(arg_keys[15], (H * HD,), (H * HD) ** -0.5, 0.125, (), jnp.float32)
    impact_vector = centred(arg_keys[16], (D,), D ** -0.5, 0.125, (), jnp.float32)
    norm_gain = jnp.clip(1.0 + 0.1 * jax.random.normal(arg_keys[17], (D,), jnp.float32), 0.5, 1.5)
    expert_gate = centred(arg_keys[18], (EXPERTS, D, FF), D ** -0.5, 0.125, ((0, 8), (2, 32)))
    expert_up = centred(arg_keys[19], (EXPERTS, D, FF), D ** -0.5, 0.125, ((0, 8), (2, 32)))
    expert_vector = centred(arg_keys[20], (EXPERTS, FF), FF ** -0.5, 0.0625, ((0, 8), (1, 32)), jnp.float32)
    routes = different_ones(arg_keys[21], NDOCS * SEQ, EXPERTS, TOP, 2048).reshape((NDOCS, SEQ, TOP))
    route_gate = jnp.clip(0.1 + 0.79999997 * jax.random.uniform(arg_keys[22], (NDOCS, SEQ, TOP), jnp.float32) ** level_of(arg_keys[22], (NDOCS, SEQ, TOP), ((0, 8), (1, 32)), -0.2, 0.2), 0.1, 0.9)
    lengths = uneven_parts(arg_keys[23], NDOCS, NDOCS * SEQ * 5 // 8, SEQ, 1).astype(jnp.int32)
    term_ids = touch_ends(ranked_ids(arg_keys[24], (NDOCS, SEQ), VOCAB, 2), jax.random.fold_in(arg_keys[24], 3), 0, VOCAB - 1).astype(jnp.int32)
    return dict(hidden=hidden, query=query, keys=keys, values=values, x_inner=x_inner, z_gate=z_gate, dt_raw=dt_raw, b_proj=b_proj, c_proj=c_proj, conv_weight=conv_weight, conv_bias=conv_bias, dt_bias=dt_bias, a_rate=a_rate, skip_gain=skip_gain, mamba_vector=mamba_vector, attn_vector=attn_vector, impact_vector=impact_vector, norm_gain=norm_gain, expert_gate=expert_gate, expert_up=expert_up, expert_vector=expert_vector, routes=routes, route_gate=route_gate, lengths=lengths, term_ids=term_ids)


big_negative = -1e+30
norm_eps = 1e-06

def attention_doc(operands):
    query_doc, key_doc, value_doc = operands
    groups = H // KVH
    score_scale = HD ** (-0.5)
    query_heads = jnp.transpose(query_doc.reshape(SEQ, H, HD), (1, 0, 2))
    key_heads = jnp.repeat(jnp.transpose(key_doc.reshape(SEQ, KVH, HD), (1, 0, 2)), groups, axis=0)
    value_heads = jnp.repeat(jnp.transpose(value_doc.reshape(SEQ, KVH, HD), (1, 0, 2)), groups, axis=0)
    positions = jnp.arange(SEQ, dtype=jnp.int32)
    allowed = positions[None, :] <= positions[:, None]

    def one_head(head_operands):
        query_one, key_one, value_one = head_operands
        scores = jnp.dot(query_one, key_one.T, preferred_element_type=jnp.float32) * score_scale
        scores = jnp.where(allowed, scores, big_negative)
        exp_scores = jnp.exp(scores - lax.optimization_barrier(jnp.max(scores, axis=-1, keepdims=True)))
        weighted = jnp.dot(exp_scores.astype(jnp.bfloat16), value_one, preferred_element_type=jnp.float32)
        return weighted / lax.optimization_barrier(jnp.sum(exp_scores, axis=-1, keepdims=True))
    heads_out = lax.map(one_head, (query_heads, key_heads, value_heads))
    return jnp.transpose(heads_out, (1, 0, 2)).reshape(SEQ, H * HD).astype(jnp.bfloat16)

def reference(hidden, query, keys, values, x_inner, z_gate, dt_raw, b_proj, c_proj, conv_weight, conv_bias, dt_bias, a_rate, skip_gain, mamba_vector, attn_vector, impact_vector, norm_gain, expert_gate, expert_up, expert_vector, routes, route_gate, lengths, term_ids):
    positions = jnp.arange(SEQ, dtype=jnp.int32)
    live_rows = positions[None, :] < lengths[:, None]
    attended = lax.map(attention_doc, (query, keys, values))
    neg_rate = -a_rate

    def mamba_doc(operands):
        inner_doc, gate_doc, raw_doc, b_doc, c_doc = operands
        padded = jnp.concatenate([jnp.zeros((KCONV - 1, INNER), jnp.float32), inner_doc.astype(jnp.float32)], axis=0)
        conv_sum = conv_bias[None, :]
        for tap_index in range(KCONV):
            conv_sum = conv_sum + conv_weight[tap_index][None, :] * padded[tap_index:tap_index + SEQ]
        conved = jax.nn.silu(conv_sum)
        step_size = jax.nn.softplus(raw_doc.astype(jnp.float32) + dt_bias[None, :])

        def emit_rows(carried, per_step):
            size_now, b_now, c_now, x_now = per_step
            carried = jnp.exp(size_now[None, :] * neg_rate) * carried + (size_now * x_now)[None, :] * b_now[:, None]
            return (carried, lax.optimization_barrier(jnp.sum(c_now[:, None] * carried, axis=0)))
        outputs = lax.scan(emit_rows, jnp.zeros(a_rate.shape, jnp.float32), (step_size, b_doc, c_doc, conved))[1]
        return ((outputs + skip_gain[None, :] * conved) * jax.nn.silu(gate_doc.astype(jnp.float32))).astype(jnp.bfloat16)
    mamba_out = lax.map(mamba_doc, (x_inner, z_gate, dt_raw, b_proj, c_proj))
    hidden_full = hidden.astype(jnp.float32)
    mean_square = lax.optimization_barrier(jnp.mean(hidden_full * hidden_full, axis=-1, keepdims=True))
    normed = (hidden_full * lax.rsqrt(mean_square + norm_eps) * norm_gain).astype(jnp.bfloat16)
    expert_ids = jnp.arange(EXPERTS, dtype=jnp.int32)
    matches = (routes[..., None] == expert_ids).astype(jnp.int32)
    chosen = lax.optimization_barrier(jnp.sum(matches, axis=2)) * live_rows[..., None].astype(jnp.int32)
    chosen_blocks = chosen.reshape(NDOCS, N_CONTEXT, TOK_DEV, EXPERTS)
    before = jnp.cumsum(chosen_blocks, axis=2) - chosen_blocks
    slot_ids = jnp.arange(CAP, dtype=jnp.int32)
    placed = ((chosen_blocks[..., None] == 1) & (before[..., None] == slot_ids)).astype(jnp.float32)
    normed_blocks = normed.reshape(NDOCS, N_CONTEXT, TOK_DEV, D).astype(jnp.float32)

    def expert_rows(operands):
        placed_one, gate_matrix, up_matrix, vector_one = operands
        gathered = jnp.einsum('dntc,dntx->dncx', placed_one, normed_blocks, precision=lax.Precision.HIGHEST)
        flat_rows = gathered.reshape(NDOCS * N_CONTEXT * CAP, D).astype(jnp.bfloat16)
        gate_part = jnp.dot(flat_rows, gate_matrix, preferred_element_type=jnp.float32)
        up_part = jnp.dot(flat_rows, up_matrix, preferred_element_type=jnp.float32)
        inner_units = (jax.nn.silu(gate_part) * up_part).astype(jnp.bfloat16)
        slot_value = lax.optimization_barrier(jnp.sum(inner_units.astype(jnp.float32) * vector_one[None, :], axis=-1))
        return slot_value.reshape(NDOCS, N_CONTEXT, CAP)
    slot_values = lax.map(expert_rows, (jnp.transpose(placed, (3, 0, 1, 2, 4)), expert_gate, expert_up, expert_vector))
    per_expert = jnp.einsum('dntec,ednc->dnte', placed, slot_values, precision=lax.Precision.HIGHEST).reshape(NDOCS, SEQ, EXPERTS)
    gate_weights = lax.optimization_barrier(jnp.sum(route_gate[..., None] * matches.astype(jnp.float32), axis=2))
    expert_score = lax.optimization_barrier(jnp.sum(per_expert * gate_weights, axis=-1))
    base_score = lax.optimization_barrier(jnp.sum(hidden_full * impact_vector, axis=-1))
    attn_score = lax.optimization_barrier(jnp.sum(attended.astype(jnp.float32) * attn_vector, axis=-1))
    mamba_score = lax.optimization_barrier(jnp.sum(mamba_out.astype(jnp.float32) * mamba_vector, axis=-1))
    score = base_score + attn_score + mamba_score + expert_score
    token_impacts = jnp.where(live_rows, jax.nn.relu(score), 0.0)

    def pool_doc(id_row, impact_row):
        return jnp.zeros((VOCAB,), jnp.float32).at[id_row].max(impact_row)
    term_impacts = jax.vmap(pool_doc)(term_ids, token_impacts)
    return (token_impacts, term_impacts)
```

```python
import jax
import jax.numpy as jnp
from jax import lax
from jax.experimental import pallas as pl
from jax.experimental.pallas import tpu as pltpu
from jax.sharding import PartitionSpec as P

H = 16
HD = 128
KVH = 4
GROUPS = H // KVH
KCONV = 4
VOCAB = 65536
D = 2048
INNER = 4096
NSTATE = 16
TOK = 128
CAP = 10
NE = 8
NCTX = 32
NY = 4
NZ = 8
FFL = 224
BLK = 512
NBLK = INNER // BLK
ROWS = NE * CAP
LOG2E = 1.4426950408889634
MESH = pl.DeviceIdType.MESH
F32 = jnp.float32
BF16 = jnp.bfloat16

NEG = -1e30
norm_eps = 1e-06


def iota(shape, axis):
    return lax.broadcasted_iota(jnp.int32, shape, axis)


def dot(a, b):
    return lax.dot_general(a, b, (((1,), (0,)), ((), ())), preferred_element_type=F32)


def dot_t(a, b):
    return lax.dot_general(a, b, (((1,), (1,)), ((), ())), preferred_element_type=F32)


def remote(src, dst, send, recv, device):
    return pltpu.make_async_remote_copy(
        src_ref=src, dst_ref=dst, send_sem=send, recv_sem=recv,
        device_id=device, device_id_type=MESH,
    )


def lane_sum(x):
    total = x[:, 0:128]
    for i in range(1, x.shape[1] // 128):
        total = total + x[:, 128 * i : 128 * (i + 1)]
    return total


def to_row(col):
    n = col.shape[0]
    eye = iota((n, 128), 0) == iota((n, 128), 1)
    return jnp.sum(jnp.where(eye, col, 0.0), axis=0, keepdims=True)


def to_col(row):
    eye = iota((128, 128), 0) == iota((128, 128), 1)
    return jnp.sum(jnp.where(eye, row, 0.0), axis=1, keepdims=True)


def kernel(
    hidden_ref, query_ref, keys_ref, values_ref, x_ref, z_ref, dtraw_ref, c_ref, a_ref,
    small_ref, ids_ref, chan_ref, feat_ref, vec_ref, w_ref,
    imp_ref, term_ref,
    wb, kb, rb, og, ar, dts, us, cvs, ext, rim, bexp, cbd, hb, pe, pr, ic, ir,
    qs, acc, ms, ls, vb, ma, zs, zr, es, er, imps, idb, lot, macc, base_s,
    lsem, ws, wr, ks, kr, vs, vr, zks, zkr, rs, rr, as_, ar_, ms_, mr_, ps, prs, qs_, qr_,
    z2s, z2r, e2s, e2r, i2s, i2r, d2s, d2r,
):
    e = lax.axis_index("expert")
    c = lax.axis_index("context")
    y = c // NZ
    z = c % NZ

    def ctx(yy, zz):
        return {"context": ((yy + NY) % NY) * NZ + (zz + NZ) % NZ}

    def cpeer(i):
        return {"context": (c + i) % NCTX}

    def epeer(i):
        return {"expert": (e + i) % NE}

    bar = pltpu.get_barrier_semaphore()

    @pl.loop(1, NCTX)
    def _(i):
        pl.semaphore_signal(bar, inc=1, device_id=cpeer(i), device_id_type=MESH)

    @pl.loop(1, NE)
    def _(i):
        pl.semaphore_signal(bar, inc=1, device_id=epeer(i), device_id_type=MESH)

    l0 = pltpu.make_async_copy(keys_ref, kb.at[z, y, :, 0:512], lsem.at[0])
    l1 = pltpu.make_async_copy(values_ref, kb.at[z, y, :, 512:1024], lsem.at[1])
    l2 = pltpu.make_async_copy(w_ref, wb.at[y], lsem.at[2])
    l0.start()
    l1.start()
    l2.start()

    hid = hidden_ref[...].astype(F32)
    mean_square = jnp.mean(hid * hid, axis=-1, keepdims=True)
    normed = (hid * lax.rsqrt(mean_square + norm_eps) * feat_ref[2:3, :]).astype(BF16)
    base_s[...] = jnp.broadcast_to(
        jnp.sum(hid * feat_ref[1:2, :], axis=-1, keepdims=True), (TOK, 128)
    )

    def routing():
        eio = iota((16, TOK), 0).astype(F32)
        m0 = small_ref[16:17, :] == eio
        m1 = small_ref[17:18, :] == eio
        live = small_ref[20:21, :]
        chosen = jnp.where(m0 | m1, live, 0.0)
        upper = jnp.where(iota((TOK, TOK), 0) < iota((TOK, TOK), 1), 1.0, 0.0).astype(BF16)
        before = dot(chosen.astype(BF16), upper)
        gates = jnp.where(m0, small_ref[18:19, :], 0.0) + jnp.where(m1, small_ref[19:20, :], 0.0)
        return chosen, before, gates

    chosen, before, _ = routing()
    sio = iota((16, TOK), 0)
    pieces = []
    for k in range(16):
        ok = (chosen[k : k + 1, :] == 1.0) & (before[k : k + 1, :] == sio.astype(F32)) & (sio < CAP)
        pieces.append(jnp.where(ok, 1.0, 0.0))
    placed = jnp.concatenate(pieces, axis=0).astype(BF16)
    og[...] = dot(placed, normed).astype(BF16).reshape(NE, 32, D)

    pl.semaphore_wait(bar, NCTX - 1 + NE - 1)
    l0.wait()
    l1.wait()
    kv_y = [remote(kb.at[z, y], kb.at[z, y], ks.at[i], kr.at[i], ctx(y + i + 1, z)) for i in range(3)]
    for k in kv_y:
        k.start()
    rim_copy = remote(x_ref.at[TOK - 16 : TOK], rim, ms_, mr_, {"context": (c + 1) % NCTX})
    rim_copy.start()

    def a2a(i):
        return remote(og.at[(e + i) % NE], ar.at[e], as_.at[i], ar_.at[i], epeer(i))

    @pl.loop(1, NE)
    def _(i):
        a2a(i).start()

    def ids_copy(i):
        return remote(ids_ref, idb.at[c], d2s.at[i], d2r.at[i], cpeer(i))

    vec_y = [remote(vec_ref, vb.at[y], vs.at[i], vr.at[i], ctx(y + i + 1, z)) for i in range(3)]
    for k in vec_y:
        k.start()
    ar[pl.ds(e, 1)] = og[pl.ds(e, 1)]
    vb[pl.ds(y, 1)] = vec_ref[...].reshape(1, 8, 512)
    idb[pl.ds(c, 1)] = ids_ref[...].reshape(1, 8, 128)

    for t in range(TOK):
        bexp[t] = jnp.broadcast_to(small_ref[0:16, t : t + 1], (16, 128))
    cf = c_ref[...]
    c_hi = cf.astype(BF16)
    c_lo = (cf - c_hi.astype(F32)).astype(BF16)
    rep = jnp.where(iota((16, 256), 0) == iota((16, 256), 1) % 16, 1.0, 0.0).astype(BF16)
    keep = (iota((TOK, 256), 1) // 16) == (iota((TOK, 256), 0) % 16)
    t_hi = jnp.where(keep, dot(c_hi, rep), 0.0).astype(BF16).reshape(8, 16, 256)
    t_lo = jnp.where(keep, dot(c_lo, rep), 0.0).astype(BF16).reshape(8, 16, 256)
    cbd[:, 0:16, :] = t_hi
    cbd[:, 16:32, :] = t_lo

    for g in range(KVH):
        for j in range(GROUPS):
            h = g * GROUPS + j
            qs[g, j * TOK : (j + 1) * TOK, :] = query_ref[:, h * HD : (h + 1) * HD]
    acc[...] = jnp.zeros_like(acc)
    ls[...] = jnp.zeros_like(ls)
    ms[...] = jnp.full_like(ms, NEG)
    ma[...] = jnp.zeros_like(ma)
    macc[...] = jnp.zeros_like(macc)
    zs[...] = jnp.zeros_like(zs)

    def zstep(buf, ss, rr_, s, half):
        bp = (z - (s - 1) + NZ) % NZ
        bm = (z + (s - 1)) % NZ
        if s < 4:
            return (
                remote(buf.at[bp], buf.at[bp], ss.at[0, s - 1], rr_.at[0, s - 1], ctx(y, z + 1)),
                remote(buf.at[bm], buf.at[bm], ss.at[1, s - 1], rr_.at[1, s - 1], ctx(y, z - 1)),
            )
        p = buf.at[bp, 0:half]
        m = buf.at[bm, half : 2 * half]
        return (
            remote(p, p, ss.at[0, s - 1], rr_.at[0, s - 1], ctx(y, z + 1)),
            remote(m, m, ss.at[1, s - 1], rr_.at[1, s - 1], ctx(y, z - 1)),
        )

    kv_step = [None] + [zstep(kb, zks, zkr, s, NY // 2) for s in range(1, 5)]
    row_step = [None] + [zstep(rb, rs, rr, s, ROWS) for s in range(1, 5)]

    def start(pair):
        for q in pair:
            q.start()

    def wait(pair):
        for q in pair:
            q.wait()

    w1 = (
        remote(wb.at[y], wb.at[y], ws.at[0], wr.at[0], ctx(y + 1, z)),
        remote(wb.at[y], wb.at[y], ws.at[1], wr.at[1], ctx(y - 1, z)),
    )
    ym = (y + NY - 1) % NY
    yp = (y + 1) % NY
    w2 = (
        remote(wb.at[ym, 0 : D // 2], wb.at[ym, 0 : D // 2], ws.at[2], wr.at[2], ctx(y + 1, z)),
        remote(wb.at[yp, D // 2 : D], wb.at[yp, D // 2 : D], ws.at[3], wr.at[3], ctx(y - 1, z)),
    )

    @pl.loop(1, NE)
    def _(i):
        a2a(i).wait()

    dst = iota((2 * ROWS, 256), 0)
    src = iota((2 * ROWS, 256), 1)
    dl, di, ds = dst // ROWS, (dst % ROWS) // CAP, dst % CAP
    pick = jnp.where(src == di * 32 + dl * 16 + ds, 1.0, 0.0).astype(BF16)
    rb[pl.ds(z, 1)] = dot(pick, ar[...].reshape(256, D)).astype(BF16).reshape(1, 2 * ROWS, D)
    start(row_step[1])
    wait(kv_y)
    start(kv_step[1])
    l2.wait()
    start(w1)

    @pl.loop(1, NCTX)
    def _(i):
        ids_copy(i).start()

    rim_copy.wait()

    @pl.loop(0, NBLK)
    def _(k):
        cols = pl.ds(pl.multiple_of(k * BLK, BLK), BLK)
        edge = jnp.where(c == 0, 0.0, rim[:, cols].astype(F32))
        ext[0:8, :] = edge[8:16, :]
        ext[8 : 8 + TOK, :] = x_ref[:, cols].astype(F32)
        for r in range(0, TOK, 32):
            rows = slice(r, r + 32)
            s = chan_ref[4:5, cols]
            for j in range(KCONV):
                s = s + chan_ref[j : j + 1, cols] * ext[r + 5 + j : r + 37 + j, :]
            cv = s / (1.0 + jnp.exp(-s))
            raw = dtraw_ref[rows, cols].astype(F32) + chan_ref[5:6, cols]
            step = jnp.maximum(raw, 0.0) + jnp.log1p(jnp.exp(-jnp.abs(raw)))
            cvs[rows, cols] = cv
            dts[rows, cols] = step
            us[rows, cols] = step * cv
        a2 = a_ref[:, cols] * (-LOG2E)

        def group(g, carried):
            h, total = carried
            base = pl.multiple_of(g * 16, 16)
            d16 = dts[pl.ds(base, 16), cols]
            u16 = us[pl.ds(base, 16), cols]
            for tt in range(16):
                b = jnp.concatenate([bexp[base + tt]] * (BLK // 128), axis=1)
                decay = jnp.exp2(a2 * d16[tt : tt + 1, :])
                h = decay * h + b * u16[tt : tt + 1, :]
            return h, total + jnp.sum(d16, axis=0, keepdims=True)

        h, total = lax.fori_loop(
            0, TOK // 16, group, (jnp.zeros((NSTATE, BLK), F32), jnp.zeros((1, BLK), F32))
        )
        for i in range(BLK // 128):
            part = jnp.concatenate(
                [h[:, 128 * i : 128 * i + 128],
                 jnp.broadcast_to(total[:, 128 * i : 128 * i + 128], (8, 128))],
                axis=0,
            )
            pe[pl.ds(k * (BLK // 128) + i, 1)] = part.reshape(1, 24, 128)

    def end_copy(i):
        return remote(pe.at[(c + i) % NCTX], pr.at[c], ps.at[i], prs.at[i], cpeer(i))

    @pl.loop(1, NCTX)
    def _(i):
        end_copy(i).start()

    pr[pl.ds(c, 1)] = pe[pl.ds(c, 1)]

    def attend(zz):
        key_pos = ((iota((TOK, 512), 1) // TOK) * NZ + zz) * TOK + iota((TOK, 512), 1) % TOK
        allowed = key_pos <= c * TOK + iota((TOK, 512), 0)
        bias = jnp.where(allowed, 0.0, NEG)

        @pl.loop(0, KVH)
        def _(g):
            kcol = pl.ds(pl.multiple_of(g * HD, HD), HD)
            vcol = pl.ds(pl.multiple_of(512 + g * HD, HD), HD)
            kk = kb[pl.ds(zz, 1), :, :, kcol].reshape(NY * TOK, HD)
            vv = kb[pl.ds(zz, 1), :, :, vcol].reshape(NY * TOK, HD)
            scores = dot_t(qs[g], kk)
            scores = (scores.reshape(GROUPS, TOK, 512) + bias[None]).reshape(GROUPS * TOK, 512)
            m_old = ms[g]
            m_new = jnp.maximum(m_old, jnp.max(scores, axis=-1, keepdims=True))
            scale = HD ** (-0.5) * LOG2E
            p = jnp.exp2((scores - jnp.concatenate([m_new] * 4, axis=1)) * scale)
            alpha = jnp.exp2((m_old - m_new) * scale)
            ls[g] = alpha * ls[g] + jnp.sum(p, axis=-1, keepdims=True)
            acc[g] = alpha * acc[g] + dot(p.astype(BF16), vv)
            ms[g] = m_new

    attend(z)

    @pl.loop(1, NCTX)
    def _(i):
        end_copy(i).wait()

    a2c = a_ref[:, pl.ds(pl.multiple_of(c * 128, 128), 128)] * (-LOG2E)

    def join(i, state):
        ic[pl.ds(i, 1)] = state.reshape(1, NSTATE, 128)
        part = pr[i]
        return jnp.exp2(a2c * part[16:17, :]) * state + part[0:16, :]

    lax.fori_loop(0, NCTX, join, jnp.zeros((NSTATE, 128), F32))

    def inc_copy(i):
        return remote(ic.at[(c + i) % NCTX], ir.at[c], qs_.at[i], qr_.at[i], cpeer(i))

    @pl.loop(1, NCTX)
    def _(i):
        inc_copy(i).start()

    ir[pl.ds(c, 1)] = ic[pl.ds(c, 1)]

    wait(row_step[1])
    start(row_step[2])
    wait(kv_step[1])
    start(kv_step[2])

    attend((z + 1) % NZ)
    attend((z + NZ - 1) % NZ)

    @pl.loop(1, NCTX)
    def _(i):
        inc_copy(i).wait()

    def second(lo, hi):
        @pl.loop(lo, hi)
        def _(k):
            cols = pl.ds(pl.multiple_of(k * BLK, BLK), BLK)
            a2 = a_ref[:, cols] * (-LOG2E)
            h0 = jnp.concatenate([ir[k * (BLK // 128) + i] for i in range(BLK // 128)], axis=1)

            def group(g, h):
                base = pl.multiple_of(g * 16, 16)
                rows = pl.ds(base, 16)
                d16 = dts[rows, cols]
                u16 = us[rows, cols]
                for tt in range(16):
                    b = jnp.concatenate([bexp[base + tt]] * (BLK // 128), axis=1)
                    decay = jnp.exp2(a2 * d16[tt : tt + 1, :])
                    h = decay * h + b * u16[tt : tt + 1, :]
                    hb[16 * tt : 16 * tt + 16, :] = h.astype(BF16)
                both = dot(cbd[g], hb[...])
                out = both[0:16, :] + both[16:32, :] + chan_ref[6:7, cols] * cvs[rows, cols]
                zg = z_ref[rows, cols].astype(F32)
                out = (out * (zg / (1.0 + jnp.exp(-zg)))).astype(BF16).astype(F32)
                macc[rows, :] += lane_sum(out * chan_ref[7:8, cols])
                return h

            lax.fori_loop(0, TOK // 16, group, h0)

    second(0, NBLK // 2)
    wait(row_step[2])
    start(row_step[3])
    second(NBLK // 2, NBLK)
    wait(kv_step[2])
    start(kv_step[3])
    attend((z + 2) % NZ)
    attend((z + NZ - 2) % NZ)

    wait(row_step[3])
    start(row_step[4])

    @pl.loop(1, NCTX)
    def _(i):
        ids_copy(i).wait()

    @pl.loop(0, NCTX)
    def _(i):
        row = idb[i][0:1, :]
        lot[pl.ds(i, 1)] = (
            jnp.where(jnp.bitwise_and(row, 127) == iota((128, 128), 0), 1.0, 0.0)
            .astype(BF16).reshape(1, 128, 128)
        )

    wait(w1)
    start(w2)
    wait(vec_y)
    wait(row_step[4])

    def experts(yb):
        for l in range(2):
            rows = rb[:, l * ROWS : (l + 1) * ROWS, :].reshape(NZ * ROWS, D)
            part = wb[pl.ds(yb, 1), :, l * 384 : l * 384 + 512].reshape(D, 512)
            both = dot(rows, part)
            up = pltpu.roll(both, 512 - FFL, 1)
            inner = ((both / (1.0 + jnp.exp(-both))) * up).astype(BF16).astype(F32)
            vec = vb[pl.ds(yb, 1)].reshape(8, 512)[l : l + 1, :]
            ma[l] += lane_sum(inner * vec)

    @pl.loop(0, 3)
    def _(i):
        experts((y + jnp.where(i == 2, NY - 1, i)) % NY)

    wait(kv_step[3])
    start(kv_step[4])
    attend((z + 3) % NZ)
    attend((z + NZ - 3) % NZ)

    wait(w2)
    experts((y + 2) % NY)

    for l in range(2):
        col = jnp.sum(ma[l], axis=1, keepdims=True)
        for q in range(NZ):
            zs[q, l : l + 1, :] = to_row(col[q * ROWS : (q + 1) * ROWS, :])

    def z_copy(i):
        return remote(zs.at[(z + i) % NZ], zr.at[z], z2s.at[i], z2r.at[i], ctx(y, z + i))

    @pl.loop(1, NZ)
    def _(i):
        z_copy(i).start()

    zr[pl.ds(z, 1)] = zs[pl.ds(z, 1)]
    wait(kv_step[4])
    attend((z + 4) % NZ)

    @pl.loop(1, NZ)
    def _(i):
        z_copy(i).wait()

    summed = zr[0]
    for q in range(1, NZ):
        summed = summed + zr[q]
    place = iota((16, 128), 0)
    es[...] = jnp.where(place == 2 * e, summed[0:1, :], 0.0) + jnp.where(
        place == 2 * e + 1, summed[1:2, :], 0.0
    )

    def e_copy(i):
        return remote(es, er.at[e], e2s.at[i], e2r.at[i], epeer(i))

    @pl.loop(1, NE)
    def _(i):
        e_copy(i).start()

    er[pl.ds(e, 1)] = es[...].reshape(1, 16, 128)

    attn = jnp.zeros((TOK, 128), F32)
    for g in range(KVH):
        ratio = (acc[g] / ls[g]).astype(BF16).astype(F32)
        for j in range(GROUPS):
            h = g * GROUPS + j
            attn = attn + ratio[j * TOK : (j + 1) * TOK, :] * feat_ref[0:1, h * HD : (h + 1) * HD]
    attn_col = jnp.sum(attn, axis=1, keepdims=True)
    mamba_col = jnp.sum(macc[...], axis=1, keepdims=True)
    own = to_row(base_s[:, 0:1] + attn_col + mamba_col)
    id_row = ids_ref[0:1, :].astype(F32)
    id_same = to_col(id_row) == id_row
    chosen, before, gates = routing()

    @pl.loop(1, NE)
    def _(i):
        e_copy(i).wait()

    back = er[0]
    for q in range(1, NE):
        back = back + er[q]
    value = jnp.zeros((16, TOK), F32)
    for s in range(CAP):
        one = jnp.sum(jnp.where(iota((16, 128), 1) == e * CAP + s, back, 0.0), axis=1, keepdims=True)
        value = value + jnp.where((chosen == 1.0) & (before == float(s)), one, 0.0)
    expert = jnp.sum(value * gates, axis=0, keepdims=True)
    impacts = small_ref[20:21, :] * jnp.maximum(own + expert, 0.0)
    imp_ref[...] = impacts

    imp_col = to_col(impacts)
    earlier = iota((TOK, TOK), 0) < iota((TOK, TOK), 1)
    beaten = id_same & ((imp_col > impacts) | ((imp_col == impacts) & earlier))
    beaten = jnp.max(jnp.where(beaten, 1.0, 0.0), axis=0, keepdims=True)
    sent = jnp.where(beaten > 0.0, 0.0, impacts)
    imps[pl.ds(c, 1)] = jnp.broadcast_to(sent, (8, 128)).reshape(1, 8, 128)

    def imp_copy(i):
        return remote(imps.at[c], imps.at[c], i2s.at[i], i2r.at[i], cpeer(i))

    @pl.loop(1, NCTX)
    def _(i):
        imp_copy(i).start()

    @pl.loop(1, NCTX)
    def _(i):
        imp_copy(i).wait()

    def pool(i, best):
        word = jnp.right_shift(idb[i][0:1, :], 7) - c * 16
        val = jnp.where(word == iota((16, 128), 0), imps[i][0:1, :], 0.0)
        p0 = val.astype(BF16)
        rest = val - p0.astype(F32)
        p1 = rest.astype(BF16)
        p2 = (rest - p1.astype(F32)).astype(BF16)
        got = dot_t(jnp.concatenate([p0, p1, p2], axis=0), lot[i])
        return jnp.maximum(best, (got[0:16] + got[16:32]) + got[32:48])

    best = lax.fori_loop(0, NCTX, pool, jnp.zeros((16, 128), F32))
    for r in range(16):
        term_ref[0:1, 128 * r : 128 * r + 128] = best[r : r + 1, :]


def shards(
    hidden, query, keys, values, x_inner, z_gate, dt_raw, b_proj, c_proj, conv_weight, conv_bias,
    dt_bias, a_rate, skip_gain, mamba_vector, attn_vector, impact_vector, norm_gain, expert_gate,
    expert_up, expert_vector, routes, route_gate, lengths, term_ids,
):
    e = lax.axis_index("expert")
    c = lax.axis_index("context")
    length = lax.dynamic_index_in_dim(lengths, e, 0, False)
    live = (c * TOK + jnp.arange(TOK, dtype=jnp.int32) < length).astype(F32)
    small = jnp.concatenate(
        [b_proj[0].T, routes[0].T.astype(F32), route_gate[0].T, live[None, :], jnp.zeros((3, TOK), F32)],
        axis=0,
    )
    ids = jnp.broadcast_to(term_ids, (8, TOK))
    chan = jnp.concatenate(
        [conv_weight, conv_bias[None], dt_bias[None], skip_gain[None], mamba_vector[None]], axis=0
    )
    feat = jnp.stack([attn_vector, impact_vector, norm_gain, norm_gain])
    weights = jnp.concatenate([expert_gate[0], expert_up[0], expert_gate[1], expert_up[1]], axis=1)
    vec = jnp.concatenate(
        [jnp.pad(expert_vector[0:1], ((0, 0), (0, 512 - FFL))),
         jnp.pad(expert_vector[1:2], ((0, 0), (64, 512 - FFL - 64))),
         jnp.zeros((6, 512), F32)],
        axis=0,
    )
    dma = pltpu.SemaphoreType.DMA
    vmem = pltpu.VMEM
    outs = pl.pallas_call(
        kernel,
        name="layers",
        out_shape=OUT_SHAPE,
        in_specs=[pl.BlockSpec(memory_space=pltpu.VMEM)] * 14 + [pl.BlockSpec(memory_space=pl.ANY)],
        out_specs=OUT_SPECS,
        scratch_shapes=[
            vmem((NY, D, 4 * FFL), BF16), vmem((NZ, NY, TOK, 1024), BF16), vmem((NZ, 2 * ROWS, D), BF16),
            vmem((NE, 32, D), BF16), vmem((NE, 32, D), BF16),
            vmem((TOK, INNER), F32), vmem((TOK, INNER), F32), vmem((TOK, INNER), F32),
            vmem((8 + TOK, BLK), F32), vmem((16, INNER), BF16), vmem((TOK, 16, 128), F32),
            vmem((8, 32, 256), BF16), vmem((256, BLK), BF16),
            vmem((NCTX, 24, 128), F32), vmem((NCTX, 24, 128), F32),
            vmem((NCTX, 16, 128), F32), vmem((NCTX, 16, 128), F32),
            vmem((KVH, GROUPS * TOK, HD), BF16), vmem((KVH, GROUPS * TOK, HD), F32),
            vmem((KVH, GROUPS * TOK, 128), F32), vmem((KVH, GROUPS * TOK, 128), F32),
            vmem((NY, 8, 512), F32), vmem((2, NZ * ROWS, 128), F32),
            vmem((NZ, 8, 128), F32), vmem((NZ, 8, 128), F32),
            vmem((16, 128), F32), vmem((NE, 16, 128), F32),
            vmem((NCTX, 8, 128), F32), vmem((NCTX, 8, 128), jnp.int32), vmem((NCTX, 128, 128), BF16),
            vmem((TOK, 128), F32), vmem((TOK, 128), F32),
            dma((3,)), dma((4,)), dma((4,)), dma((3,)), dma((3,)), dma((3,)), dma((3,)),
            dma((2, 4)), dma((2, 4)), dma((2, 4)), dma((2, 4)), dma((NE,)), dma((NE,)), dma, dma,
            dma((NCTX,)), dma((NCTX,)), dma((NCTX,)), dma((NCTX,)),
            dma((NZ,)), dma((NZ,)), dma((NE,)), dma((NE,)), dma((NCTX,)), dma((NCTX,)),
            dma((NCTX,)), dma((NCTX,)),
        ],
        compiler_params=pltpu.CompilerParams(
            collective_id=0, has_side_effects=True, vmem_limit_bytes=VMEM_LIMIT
        ),
    )(
        hidden[0], query[0], keys[0], values[0], x_inner[0], z_gate[0], dt_raw[0], c_proj[0], a_rate,
        small, ids, chan, feat, vec, weights,
    )
    return tuple(outs)


OUT_SHAPE = (jax.ShapeDtypeStruct((1, TOK), F32), jax.ShapeDtypeStruct((1, VOCAB // NCTX), F32))
OUT_SPECS = (pl.BlockSpec(memory_space=pltpu.VMEM),) * 2
VMEM_LIMIT = 63 << 20


def solution(mesh):
    doc = P("expert", "context", None)
    placed = (doc,) * 9 + (P(),) * 9 + (
        P("expert", None, "context"),
        P("expert", None, "context"),
        P("expert", "context"),
        doc,
        doc,
        P(),
        P("expert", "context"),
    )
    return jax.shard_map(
        shards,
        mesh=mesh,
        in_specs=placed,
        out_specs=(P("expert", "context"), P("expert", "context")),
        check_vma=False,
    )
```

```python
import jax
import jax.numpy as jnp
from jax import lax
from jax.experimental import pallas as pl
from jax.experimental.pallas import tpu as pltpu
from jax.sharding import PartitionSpec as P

H = 16
HD = 128
KVH = 4
GROUPS = H // KVH
KCONV = 4
VOCAB = 65536
D = 2048
INNER = 4096
NSTATE = 16
TOK = 128
CAP = 10
NE = 8
NCTX = 32
NY = 4
NZ = 8
FFL = 224
BLK = 512
NBLK = INNER // BLK
ROWS = NE * CAP
LOG2E = 1.4426950408889634
MESH = pl.DeviceIdType.MESH
F32 = jnp.float32
BF16 = jnp.bfloat16

NEG = -1e30
norm_eps = 1e-06


def iota(shape, axis):
    return lax.broadcasted_iota(jnp.int32, shape, axis)


def dot(a, b):
    return lax.dot_general(a, b, (((1,), (0,)), ((), ())), preferred_element_type=F32)


def dot_t(a, b):
    return lax.dot_general(a, b, (((1,), (1,)), ((), ())), preferred_element_type=F32)


def dot_l(a, b):
    return lax.dot_general(a, b, (((0,), (0,)), ((), ())), preferred_element_type=F32)


def remote(src, dst, send, recv, device):
    return pltpu.make_async_remote_copy(
        src_ref=src, dst_ref=dst, send_sem=send, recv_sem=recv,
        device_id=device, device_id_type=MESH,
    )


def lane_sum(x):
    total = x[:, 0:128]
    for i in range(1, x.shape[1] // 128):
        total = total + x[:, 128 * i : 128 * (i + 1)]
    return total


def to_row(col):
    n = col.shape[0]
    eye = iota((n, 128), 0) == iota((n, 128), 1)
    return jnp.sum(jnp.where(eye, col, 0.0), axis=0, keepdims=True)


def to_col(row):
    eye = iota((128, 128), 0) == iota((128, 128), 1)
    return jnp.sum(jnp.where(eye, row, 0.0), axis=1, keepdims=True)


def kernel(
    hidden_ref, query_ref, keys_ref, values_ref, x_ref, z_ref, dtraw_ref, c_ref, a_ref,
    b_ref, routes_ref, gates_ref, len_ref, terms_ref, taps_ref, cbias_ref, dbias_ref, skip_ref, mvec_ref,
    avec_ref, ivec_ref, gain_ref, evec_ref, gate_ref, up_ref,
    imp_ref, term_ref,
    wb, kb, rb, og, ar, dts, us, cvs, ext, rim, bexp, cbd, hb, pe, pr, ic, ir,
    qs, acc, ms, ls, vb, ma, zs, zr, es, er, imps, idb, lot, macc, base_s,
    lsem, ws, wr, ks, kr, vs, vr, zos, zor, zks, zkr, rs, rr, as_, ar_, ms_, mr_, ps, prs, qs_, qr_,
    z2s, z2r, e2s, e2r, i2s, i2r, d2s, d2r,
):
    e = lax.axis_index("expert")
    c = lax.axis_index("context")
    y = c // NZ
    z = c % NZ

    def ctx(yy, zz):
        return {"context": ((yy + NY) % NY) * NZ + (zz + NZ) % NZ}

    def cpeer(i):
        return {"context": (c + i) % NCTX}

    def epeer(i):
        return {"expert": (e + i) % NE}

    bar = pltpu.get_barrier_semaphore()

    @pl.loop(1, NCTX)
    def _(i):
        pl.semaphore_signal(bar, inc=1, device_id=cpeer(i), device_id_type=MESH)

    @pl.loop(1, NE)
    def _(i):
        pl.semaphore_signal(bar, inc=1, device_id=epeer(i), device_id_type=MESH)

    l0 = pltpu.make_async_copy(keys_ref, kb.at[z, 0, :, 0:512], lsem.at[0])
    l1 = pltpu.make_async_copy(values_ref, kb.at[z, 0, :, 512:1024], lsem.at[1])
    load_w = []
    for l in range(2):
        at = 2 * FFL * l
        load_w.append(pltpu.make_async_copy(gate_ref.at[l], wb.at[y, at : at + FFL], lsem.at[2 + 2 * l]))
        at = at + FFL
        load_w.append(pltpu.make_async_copy(up_ref.at[l], wb.at[y, at : at + FFL], lsem.at[3 + 2 * l]))
    l0.start()
    l1.start()
    for k in load_w:
        k.start()

    def zstep(view, ss, rr_, s):
        bp = (z - (s - 1) + NZ) % NZ
        bm = (z + (s - 1)) % NZ
        p, m = view(bp, 0 if s == 4 else None), view(bm, 1 if s == 4 else None)
        return (
            remote(p, p, ss.at[0, s - 1], rr_.at[0, s - 1], ctx(y, z + 1)),
            remote(m, m, ss.at[1, s - 1], rr_.at[1, s - 1], ctx(y, z - 1)),
        )

    def own_view(b, half):
        if half is None:
            return kb.at[b, 0]
        return kb.at[b, 0, half * 64 : half * 64 + 64]

    def kv_view(b, half):
        if half is None:
            return kb.at[b, 1:NY]
        return kb.at[b, 1:NY, half * 64 : half * 64 + 64]

    def row_view(b, half):
        if half is None:
            return rb.at[b]
        return rb.at[b, half * ROWS : (half + 1) * ROWS]

    own_step = [None] + [zstep(own_view, zos, zor, s) for s in range(1, 5)]
    kv_step = [None] + [zstep(kv_view, zks, zkr, s) for s in range(1, 5)]
    row_step = [None] + [zstep(row_view, rs, rr, s) for s in range(1, 5)]

    def start(pair):
        for q in pair:
            q.start()

    def wait(pair):
        for q in pair:
            q.wait()

    def w1(q):
        own = wb.at[y, q * FFL : (q + 1) * FFL]
        return (
            remote(own, own, ws.at[0, q], wr.at[0, q], ctx(y + 1, z)),
            remote(own, own, ws.at[1, q], wr.at[1, q], ctx(y - 1, z)),
        )

    ym = (y + NY - 1) % NY
    yp = (y + 1) % NY
    w2 = (
        remote(wb.at[ym, 0 : 2 * FFL], wb.at[ym, 0 : 2 * FFL], ws.at[0, 4], wr.at[0, 4], ctx(y + 1, z)),
        remote(wb.at[yp, 2 * FFL : 4 * FFL], wb.at[yp, 2 * FFL : 4 * FFL], ws.at[1, 4], wr.at[1, 4], ctx(y - 1, z)),
    )

    idb[pl.ds(c, 1)] = terms_ref[...].reshape(1, 1, TOK)
    vb[pl.ds(y, 1), 0:2, :] = evec_ref[...].reshape(1, 2, FFL)
    l0.wait()
    l1.wait()
    pl.semaphore_wait(bar, NCTX - 1 + NE - 1)
    rim_copy = remote(x_ref.at[TOK - 16 : TOK], rim, ms_, mr_, {"context": (c + 1) % NCTX})
    rim_copy.start()
    vec_y = [remote(vb.at[y], vb.at[y], vs.at[i], vr.at[i], ctx(y + i + 1, z)) for i in range(3)]
    start(own_step[1])
    start(vec_y)
    kv_y = [remote(kb.at[z, 0], kb.at[z, 3 - i], ks.at[i], kr.at[i], ctx(y + i + 1, z)) for i in range(3)]
    start(kv_y)

    def ids_copy(i):
        return remote(idb.at[c], idb.at[c], d2s.at[i], d2r.at[i], cpeer(i))

    @pl.loop(1, NCTX)
    def _(i):
        ids_copy(i).start()

    wait(load_w)
    start(w1(0))
    start(w1(1))

    hid = hidden_ref[...].astype(F32)
    mean_square = jnp.mean(hid * hid, axis=-1, keepdims=True)
    normed = (hid * lax.rsqrt(mean_square + norm_eps) * gain_ref[...]).astype(BF16)
    base_s[...] = jnp.broadcast_to(
        jnp.sum(hid * ivec_ref[...], axis=-1, keepdims=True), (TOK, 128)
    )

    live = (c * TOK + iota((1, TOK), 1) < len_ref[e]).astype(F32)
    r0, r1 = routes_ref[0:1, :].astype(F32), routes_ref[1:2, :].astype(F32)
    g0, g1 = gates_ref[0:1, :], gates_ref[1:2, :]
    b_rows = b_ref[...]

    def routing():
        eio = iota((16, TOK), 0).astype(F32)
        m0 = r0 == eio
        m1 = r1 == eio
        chosen = jnp.where(m0 | m1, live, 0.0)
        upper = jnp.where(iota((TOK, TOK), 0) < iota((TOK, TOK), 1), 1.0, 0.0).astype(BF16)
        before = dot(chosen.astype(BF16), upper)
        gates = jnp.where(m0, g0, 0.0) + jnp.where(m1, g1, 0.0)
        return chosen, before, gates

    chosen, before, _ = routing()
    sio = iota((16, TOK), 0)
    pieces = []
    for k in range(16):
        ok = (chosen[k : k + 1, :] == 1.0) & (before[k : k + 1, :] == sio.astype(F32)) & (sio < CAP)
        pieces.append(jnp.where(ok, 1.0, 0.0))
    placed = jnp.concatenate(pieces, axis=0).astype(BF16)
    og[...] = dot(placed, normed).astype(BF16).reshape(NE, 32, D)


    def a2a(i):
        return remote(og.at[(e + i) % NE], ar.at[e], as_.at[i], ar_.at[i], epeer(i))

    @pl.loop(1, NE)
    def _(i):
        a2a(i).start()

    ar[pl.ds(e, 1)] = og[pl.ds(e, 1)]

    for t in range(TOK):
        bexp[t] = jnp.broadcast_to(b_rows[:, t : t + 1], (16, 128))
    cf = c_ref[...]
    c_hi = cf.astype(BF16)
    c_lo = (cf - c_hi.astype(F32)).astype(BF16)
    rep = jnp.where(iota((16, 256), 0) == iota((16, 256), 1) % 16, 1.0, 0.0).astype(BF16)
    keep = (iota((TOK, 256), 1) // 16) == (iota((TOK, 256), 0) % 16)
    t_hi = jnp.where(keep, dot_l(c_hi, rep), 0.0).astype(BF16).reshape(8, 16, 256)
    t_lo = jnp.where(keep, dot_l(c_lo, rep), 0.0).astype(BF16).reshape(8, 16, 256)
    cbd[:, 0:16, :] = t_hi
    cbd[:, 16:32, :] = t_lo

    for g in range(KVH):
        for j in range(GROUPS):
            h = g * GROUPS + j
            qs[g, j * TOK : (j + 1) * TOK, :] = query_ref[:, h * HD : (h + 1) * HD]
    acc[...] = jnp.zeros_like(acc)
    ls[...] = jnp.zeros_like(ls)
    ms[...] = jnp.full_like(ms, NEG)
    ma[...] = jnp.zeros_like(ma)
    macc[...] = jnp.zeros_like(macc)
    zs[...] = jnp.zeros_like(zs)

    wait(kv_y)
    start(kv_step[1])
    wait(own_step[1])
    start(own_step[2])

    @pl.loop(1, NE)
    def _(i):
        a2a(i).wait()

    dst = iota((2 * ROWS, 256), 0)
    src = iota((2 * ROWS, 256), 1)
    dl, di, ds = dst // ROWS, (dst % ROWS) // CAP, dst % CAP
    pick = jnp.where(src == di * 32 + dl * 16 + ds, 1.0, 0.0).astype(BF16)
    rb[pl.ds(z, 1)] = dot(pick, ar[...].reshape(256, D)).astype(BF16).reshape(1, 2 * ROWS, D)
    start(row_step[1])
    wait(own_step[2])
    start(own_step[3])
    rim_copy.wait()

    @pl.loop(0, NBLK)
    def _(k):
        cols = pl.ds(pl.multiple_of(k * BLK, BLK), BLK)
        edge = jnp.where(c == 0, 0.0, rim[:, cols].astype(F32))
        ext[0:8, :] = edge[8:16, :]
        ext[8 : 8 + TOK, :] = x_ref[:, cols].astype(F32)
        for r in range(0, TOK, 32):
            rows = slice(r, r + 32)
            s = cbias_ref[0:1, cols]
            for j in range(KCONV):
                s = s + taps_ref[j : j + 1, cols] * ext[r + 5 + j : r + 37 + j, :]
            cv = s / (1.0 + jnp.exp(-s))
            raw = dtraw_ref[rows, cols].astype(F32) + dbias_ref[0:1, cols]
            step = jnp.maximum(raw, 0.0) + jnp.log1p(jnp.exp(-jnp.abs(raw)))
            cvs[rows, cols] = cv
            dts[rows, cols] = step
            us[rows, cols] = step * cv
        a2 = a_ref[:, cols] * (-LOG2E)

        def group(g, carried):
            h, total = carried
            base = pl.multiple_of(g * 16, 16)
            d16 = dts[pl.ds(base, 16), cols]
            u16 = us[pl.ds(base, 16), cols]
            for tt in range(16):
                b = jnp.concatenate([bexp[base + tt]] * (BLK // 128), axis=1)
                decay = jnp.exp2(a2 * d16[tt : tt + 1, :])
                h = decay * h + b * u16[tt : tt + 1, :]
            return h, total + jnp.sum(d16, axis=0, keepdims=True)

        h, total = lax.fori_loop(
            0, TOK // 16, group, (jnp.zeros((NSTATE, BLK), F32), jnp.zeros((1, BLK), F32))
        )
        for i in range(BLK // 128):
            part = jnp.concatenate(
                [h[:, 128 * i : 128 * i + 128],
                 jnp.broadcast_to(total[:, 128 * i : 128 * i + 128], (8, 128))],
                axis=0,
            )
            pe[pl.ds(k * (BLK // 128) + i, 1)] = part.reshape(1, 24, 128)

    def end_copy(i):
        return remote(pe.at[(c + i) % NCTX], pr.at[c], ps.at[i], prs.at[i], cpeer(i))

    @pl.loop(1, NCTX)
    def _(i):
        end_copy(i).start()

    pr[pl.ds(c, 1)] = pe[pl.ds(c, 1)]

    start(w1(2))

    def attend(zz):
        key_pos = (((iota((TOK, 512), 1) // TOK + y) % NY) * NZ + zz) * TOK + iota((TOK, 512), 1) % TOK
        allowed = key_pos <= c * TOK + iota((TOK, 512), 0)
        bias = jnp.where(allowed, 0.0, NEG)

        @pl.loop(0, KVH)
        def _(g):
            kcol = pl.ds(pl.multiple_of(g * HD, HD), HD)
            vcol = pl.ds(pl.multiple_of(512 + g * HD, HD), HD)
            kk = kb[pl.ds(zz, 1), :, :, kcol].reshape(NY * TOK, HD)
            vv = kb[pl.ds(zz, 1), :, :, vcol].reshape(NY * TOK, HD)
            scores = dot_t(qs[g], kk)
            scores = (scores.reshape(GROUPS, TOK, 512) + bias[None]).reshape(GROUPS * TOK, 512)
            m_old = ms[g]
            m_new = jnp.maximum(m_old, jnp.max(scores, axis=-1, keepdims=True))
            scale = HD ** (-0.5) * LOG2E
            p = jnp.exp2((scores - jnp.concatenate([m_new] * 4, axis=1)) * scale)
            alpha = jnp.exp2((m_old - m_new) * scale)
            ls[g] = alpha * ls[g] + jnp.sum(p, axis=-1, keepdims=True)
            acc[g] = alpha * acc[g] + dot(p.astype(BF16), vv)
            ms[g] = m_new

    attend(z)
    wait(own_step[3])
    start(own_step[4])
    wait(row_step[1])
    start(row_step[2])
    wait(kv_step[1])
    start(kv_step[2])
    attend((z + 1) % NZ)
    attend((z + NZ - 1) % NZ)

    @pl.loop(1, NCTX)
    def _(i):
        end_copy(i).wait()

    a2c = a_ref[:, pl.ds(pl.multiple_of(c * 128, 128), 128)] * (-LOG2E)

    def join(i, state):
        ic[pl.ds(i, 1)] = state.reshape(1, NSTATE, 128)
        part = pr[i]
        return jnp.exp2(a2c * part[16:17, :]) * state + part[0:16, :]

    lax.fori_loop(0, NCTX, join, jnp.zeros((NSTATE, 128), F32))

    def inc_copy(i):
        return remote(ic.at[(c + i) % NCTX], ir.at[c], qs_.at[i], qr_.at[i], cpeer(i))

    @pl.loop(1, NCTX)
    def _(i):
        inc_copy(i).start()

    ir[pl.ds(c, 1)] = ic[pl.ds(c, 1)]

    start(w1(3))

    @pl.loop(1, NCTX)
    def _(i):
        ids_copy(i).wait()

    @pl.loop(0, NCTX)
    def _(i):
        row = idb[i][0:1, :]
        lot[pl.ds(i, 1)] = (
            jnp.where(jnp.bitwise_and(row, 127) == iota((128, 128), 0), 1.0, 0.0)
            .astype(BF16).reshape(1, 128, 128)
        )

    def second(lo, hi):
        @pl.loop(lo, hi)
        def _(k):
            cols = pl.ds(pl.multiple_of(k * BLK, BLK), BLK)
            a2 = a_ref[:, cols] * (-LOG2E)
            h0 = jnp.concatenate([ir[k * (BLK // 128) + i] for i in range(BLK // 128)], axis=1)

            def group(g, h):
                base = pl.multiple_of(g * 16, 16)
                rows = pl.ds(base, 16)
                d16 = dts[rows, cols]
                u16 = us[rows, cols]
                for tt in range(16):
                    b = jnp.concatenate([bexp[base + tt]] * (BLK // 128), axis=1)
                    decay = jnp.exp2(a2 * d16[tt : tt + 1, :])
                    h = decay * h + b * u16[tt : tt + 1, :]
                    hb[16 * tt : 16 * tt + 16, :] = h.astype(BF16)
                both = dot(cbd[g], hb[...])
                out = both[0:16, :] + both[16:32, :] + skip_ref[0:1, cols] * cvs[rows, cols]
                zg = z_ref[rows, cols].astype(F32)
                out = (out * (zg / (1.0 + jnp.exp(-zg)))).astype(BF16).astype(F32)
                macc[rows, :] += lane_sum(out * mvec_ref[0:1, cols])
                return h

            lax.fori_loop(0, TOK // 16, group, h0)

    def experts(yb):
        for l in range(2):
            rows = rb[:, l * ROWS : (l + 1) * ROWS, :].reshape(NZ * ROWS, D)
            gate = dot_t(rows, wb[pl.ds(yb, 1), 2 * l * FFL : (2 * l + 1) * FFL, :].reshape(FFL, D))
            up = dot_t(rows, wb[pl.ds(yb, 1), (2 * l + 1) * FFL : (2 * l + 2) * FFL, :].reshape(FFL, D))
            inner = ((gate / (1.0 + jnp.exp(-gate))) * up).astype(BF16).astype(F32)
            term = inner * vb[pl.ds(yb, 1)].reshape(8, FFL)[l : l + 1, :]
            ma[l] += jnp.sum(term, axis=1, keepdims=True)

    wait(row_step[2])
    start(row_step[3])
    wait(kv_step[2])
    start(kv_step[3])
    for q in range(4):
        wait(w1(q))
    start(w2)
    @pl.loop(1, NCTX)
    def _(i):
        inc_copy(i).wait()

    second(0, NBLK // 2)
    wait(row_step[3])
    start(row_step[4])
    second(NBLK // 2, NBLK)
    attend((z + 2) % NZ)
    attend((z + NZ - 2) % NZ)
    wait(kv_step[3])
    start(kv_step[4])
    wait(vec_y)
    wait(row_step[4])

    @pl.loop(0, 3)
    def _(i):
        experts((y + jnp.where(i == 2, NY - 1, i)) % NY)

    attend((z + 3) % NZ)
    attend((z + NZ - 3) % NZ)
    wait(w2)
    experts((y + 2) % NY)

    for l in range(2):
        col = ma[l][:, 0:1]
        for q in range(NZ):
            zs[q, l : l + 1, :] = to_row(col[q * ROWS : (q + 1) * ROWS, :])

    def z_copy(i):
        return remote(zs.at[(z + i) % NZ], zr.at[z], z2s.at[i], z2r.at[i], ctx(y, z + i))

    @pl.loop(1, NZ)
    def _(i):
        z_copy(i).start()

    zr[pl.ds(z, 1)] = zs[pl.ds(z, 1)]
    wait(own_step[4])
    wait(kv_step[4])
    attend((z + 4) % NZ)

    @pl.loop(1, NZ)
    def _(i):
        z_copy(i).wait()

    summed = zr[0]
    for q in range(1, NZ):
        summed = summed + zr[q]
    place = iota((16, 128), 0)
    es[...] = jnp.where(place == 2 * e, summed[0:1, :], 0.0) + jnp.where(
        place == 2 * e + 1, summed[1:2, :], 0.0
    )

    def e_copy(i):
        return remote(es, er.at[e], e2s.at[i], e2r.at[i], epeer(i))

    @pl.loop(1, NE)
    def _(i):
        e_copy(i).start()

    er[pl.ds(e, 1)] = es[...].reshape(1, 16, 128)

    attn = jnp.zeros((TOK, 128), F32)
    for g in range(KVH):
        ratio = (acc[g] / ls[g]).astype(BF16).astype(F32)
        for j in range(GROUPS):
            h = g * GROUPS + j
            attn = attn + ratio[j * TOK : (j + 1) * TOK, :] * avec_ref[0:1, h * HD : (h + 1) * HD]
    attn_col = jnp.sum(attn, axis=1, keepdims=True)
    mamba_col = jnp.sum(macc[...], axis=1, keepdims=True)
    own = to_row(base_s[:, 0:1] + attn_col + mamba_col)
    id_row = terms_ref[...].astype(F32)
    id_same = to_col(id_row) == id_row
    chosen, before, gates = routing()

    @pl.loop(1, NE)
    def _(i):
        e_copy(i).wait()

    back = er[0]
    for q in range(1, NE):
        back = back + er[q]
    value = jnp.zeros((16, TOK), F32)
    for s in range(CAP):
        one = jnp.sum(jnp.where(iota((16, 128), 1) == e * CAP + s, back, 0.0), axis=1, keepdims=True)
        value = value + jnp.where((chosen == 1.0) & (before == float(s)), one, 0.0)
    expert = jnp.sum(value * gates, axis=0, keepdims=True)
    impacts = live * jnp.maximum(own + expert, 0.0)
    imp_ref[...] = impacts

    imp_col = to_col(impacts)
    earlier = iota((TOK, TOK), 0) < iota((TOK, TOK), 1)
    beaten = id_same & ((imp_col > impacts) | ((imp_col == impacts) & earlier))
    beaten = jnp.max(jnp.where(beaten, 1.0, 0.0), axis=0, keepdims=True)
    sent = jnp.where(beaten > 0.0, 0.0, impacts)
    imps[pl.ds(c, 1)] = sent.reshape(1, 1, 128)

    def imp_copy(i):
        return remote(imps.at[c], imps.at[c], i2s.at[i], i2r.at[i], cpeer(i))

    @pl.loop(1, NCTX)
    def _(i):
        imp_copy(i).start()

    @pl.loop(1, NCTX)
    def _(i):
        imp_copy(i).wait()

    def pool(i, best):
        word = jnp.right_shift(idb[i][0:1, :], 7) - c * 16
        val = jnp.where(word == iota((16, 128), 0), imps[i][0:1, :], 0.0)
        p0 = val.astype(BF16)
        rest = val - p0.astype(F32)
        p1 = rest.astype(BF16)
        p2 = (rest - p1.astype(F32)).astype(BF16)
        got = dot_t(jnp.concatenate([p0, p1, p2], axis=0), lot[i])
        return jnp.maximum(best, (got[0:16] + got[16:32]) + got[32:48])

    best = lax.fori_loop(0, NCTX, pool, jnp.zeros((16, 128), F32))
    for r in range(16):
        term_ref[0:1, 128 * r : 128 * r + 128] = best[r : r + 1, :]


def shards(
    hidden, query, keys, values, x_inner, z_gate, dt_raw, b_proj, c_proj, conv_weight, conv_bias,
    dt_bias, a_rate, skip_gain, mamba_vector, attn_vector, impact_vector, norm_gain, expert_gate,
    expert_up, expert_vector, routes, route_gate, lengths, term_ids,
):
    dma = pltpu.SemaphoreType.DMA
    vmem = pltpu.VMEM
    outs = pl.pallas_call(
        kernel,
        name="layers",
        out_shape=OUT_SHAPE,
        in_specs=[pl.BlockSpec(memory_space=pltpu.VMEM)] * 12
        + [pl.BlockSpec(memory_space=pltpu.SMEM)]
        + [pl.BlockSpec(memory_space=pltpu.VMEM)] * 10
        + [pl.BlockSpec(memory_space=pl.ANY)] * 2,
        out_specs=OUT_SPECS,
        scratch_shapes=[
            vmem((NY, 4 * FFL, D), BF16), vmem((NZ, NY, TOK, 1024), BF16), vmem((NZ, 2 * ROWS, D), BF16),
            vmem((NE, 32, D), BF16), vmem((NE, 32, D), BF16),
            vmem((TOK, INNER), F32), vmem((TOK, INNER), F32), vmem((TOK, INNER), F32),
            vmem((8 + TOK, BLK), F32), vmem((16, INNER), BF16), vmem((TOK, 16, 128), F32),
            vmem((8, 32, 256), BF16), vmem((256, BLK), BF16),
            vmem((NCTX, 24, 128), F32), vmem((NCTX, 24, 128), F32),
            vmem((NCTX, 16, 128), F32), vmem((NCTX, 16, 128), F32),
            vmem((KVH, GROUPS * TOK, HD), BF16), vmem((KVH, GROUPS * TOK, HD), F32),
            vmem((KVH, GROUPS * TOK, 128), F32), vmem((KVH, GROUPS * TOK, 128), F32),
            vmem((NY, 8, FFL), F32), vmem((2, NZ * ROWS, 128), F32),
            vmem((NZ, 8, 128), F32), vmem((NZ, 8, 128), F32),
            vmem((16, 128), F32), vmem((NE, 16, 128), F32),
            vmem((NCTX, 1, 128), F32), vmem((NCTX, 1, 128), jnp.int32), vmem((NCTX, 128, 128), BF16),
            vmem((TOK, 128), F32), vmem((TOK, 128), F32),
            dma((6,)), dma((2, 5)), dma((2, 5)), dma((3,)), dma((3,)), dma((3,)), dma((3,)),
            dma((2, 4)), dma((2, 4)), dma((2, 4)), dma((2, 4)), dma((2, 4)), dma((2, 4)), dma((NE,)), dma((NE,)), dma, dma,
            dma((NCTX,)), dma((NCTX,)), dma((NCTX,)), dma((NCTX,)),
            dma((NZ,)), dma((NZ,)), dma((NE,)), dma((NE,)), dma((NCTX,)), dma((NCTX,)),
            dma((NCTX,)), dma((NCTX,)),
        ],
        compiler_params=pltpu.CompilerParams(
            collective_id=0, has_side_effects=True, vmem_limit_bytes=VMEM_LIMIT
        ),
    )(
        hidden[0], query[0], keys[0], values[0], x_inner[0], z_gate[0], dt_raw[0], c_proj[0].T, a_rate,
        b_proj[0].T, routes[0].T, route_gate[0].T, lengths, term_ids, conv_weight, conv_bias[None],
        dt_bias[None], skip_gain[None], mamba_vector[None], attn_vector[None], impact_vector[None],
        norm_gain[None], expert_vector, jnp.swapaxes(expert_gate, 1, 2), jnp.swapaxes(expert_up, 1, 2),
    )
    return tuple(outs)


OUT_SHAPE = (jax.ShapeDtypeStruct((1, TOK), F32), jax.ShapeDtypeStruct((1, VOCAB // NCTX), F32))
OUT_SPECS = (pl.BlockSpec(memory_space=pltpu.VMEM),) * 2
VMEM_LIMIT = 63 << 20


def solution(mesh):
    doc = P("expert", "context", None)
    placed = (doc,) * 9 + (P(),) * 9 + (
        P("expert", None, "context"),
        P("expert", None, "context"),
        P("expert", "context"),
        doc,
        doc,
        P(),
        P("expert", "context"),
    )
    return jax.shard_map(
        shards,
        mesh=mesh,
        in_specs=placed,
        out_specs=(P("expert", "context"), P("expert", "context")),
        check_vma=False,
    )
```

```python
import jax
import jax.numpy as jnp
from jax import lax
from jax.experimental import pallas as pl
from jax.experimental.pallas import tpu as pltpu
from jax.sharding import PartitionSpec as P

H = 16
HD = 128
KVH = 4
GROUPS = H // KVH
KCONV = 4
VOCAB = 65536
D = 2048
INNER = 4096
NSTATE = 16
TOK = 128
CAP = 10
NE = 8
NCTX = 32
NY = 4
NZ = 8
FFL = 224
BLK = 512
NBLK = INNER // BLK
ROWS = NE * CAP
LOG2E = 1.4426950408889634
MESH = pl.DeviceIdType.MESH
F32 = jnp.float32
BF16 = jnp.bfloat16

NEG = -1e30
norm_eps = 1e-06


def iota(shape, axis):
    return lax.broadcasted_iota(jnp.int32, shape, axis)


def dot(a, b):
    return lax.dot_general(a, b, (((1,), (0,)), ((), ())), preferred_element_type=F32)


def dot_t(a, b):
    return lax.dot_general(a, b, (((1,), (1,)), ((), ())), preferred_element_type=F32)


def dot_l(a, b):
    return lax.dot_general(a, b, (((0,), (0,)), ((), ())), preferred_element_type=F32)


def remote(src, dst, send, recv, device):
    return pltpu.make_async_remote_copy(
        src_ref=src, dst_ref=dst, send_sem=send, recv_sem=recv,
        device_id=device, device_id_type=MESH,
    )


def lane_sum(x):
    total = x[:, 0:128]
    for i in range(1, x.shape[1] // 128):
        total = total + x[:, 128 * i : 128 * (i + 1)]
    return total


def to_row(col):
    n = col.shape[0]
    eye = iota((n, 128), 0) == iota((n, 128), 1)
    return jnp.sum(jnp.where(eye, col, 0.0), axis=0, keepdims=True)


def to_col(row):
    eye = iota((128, 128), 0) == iota((128, 128), 1)
    return jnp.sum(jnp.where(eye, row, 0.0), axis=1, keepdims=True)


def kernel(
    hidden_ref, query_ref, keys_ref, values_ref, x_ref, z_ref, dtraw_ref, c_ref, a_ref,
    b_ref, routes_ref, gates_ref, len_ref, terms_ref, taps_ref, cbias_ref, dbias_ref, skip_ref, mvec_ref,
    avec_ref, ivec_ref, gain_ref, evec_ref, gate_ref, up_ref,
    imp_ref, term_ref,
    wb, kb, rb, og, ar, dts, us, cvs, ext, rim, bexp, cbd, hb, pe, pr, ic, ir,
    qs, acc, ms, ls, vb, ma, zs, zr, es, er, imps, idb, lot, macc, base_s,
    lsem, ws, wr, ks, kr, vs, vr, zos, zor, zks, zkr, rs, rr, as_, ar_, ms_, mr_, ps, prs, qs_, qr_,
    z2s, z2r, e2s, e2r, i2s, i2r, d2s, d2r,
):
    e = lax.axis_index("expert")
    c = lax.axis_index("context")
    y = c // NZ
    z = c % NZ

    def ctx(yy, zz):
        return {"context": ((yy + NY) % NY) * NZ + (zz + NZ) % NZ}

    def cpeer(i):
        return {"context": (c + i) % NCTX}

    def epeer(i):
        return {"expert": (e + i) % NE}

    bar = pltpu.get_barrier_semaphore()

    @pl.loop(1, NCTX)
    def _(i):
        pl.semaphore_signal(bar, inc=1, device_id=cpeer(i), device_id_type=MESH)

    @pl.loop(1, NE)
    def _(i):
        pl.semaphore_signal(bar, inc=1, device_id=epeer(i), device_id_type=MESH)

    l0 = pltpu.make_async_copy(keys_ref, kb.at[z, 0, :, 0:512], lsem.at[0])
    l1 = pltpu.make_async_copy(values_ref, kb.at[z, 0, :, 512:1024], lsem.at[1])
    load_w = []
    for l in range(2):
        at = 2 * FFL * l
        load_w.append(pltpu.make_async_copy(gate_ref.at[l], wb.at[y, at : at + FFL], lsem.at[2 + 2 * l]))
        at = at + FFL
        load_w.append(pltpu.make_async_copy(up_ref.at[l], wb.at[y, at : at + FFL], lsem.at[3 + 2 * l]))
    l0.start()
    l1.start()
    for k in load_w:
        k.start()

    def zstep(view, ss, rr_, s):
        bp = (z - (s - 1) + NZ) % NZ
        bm = (z + (s - 1)) % NZ
        p, m = view(bp, 0 if s == 4 else None), view(bm, 1 if s == 4 else None)
        return (
            remote(p, p, ss.at[0, s - 1], rr_.at[0, s - 1], ctx(y, z + 1)),
            remote(m, m, ss.at[1, s - 1], rr_.at[1, s - 1], ctx(y, z - 1)),
        )

    def own_view(b, half):
        if half is None:
            return kb.at[b, 0]
        return kb.at[b, 0, half * 64 : half * 64 + 64]

    def kv_view(b, half):
        if half is None:
            return kb.at[b, 1:NY]
        return kb.at[b, 1:NY, half * 64 : half * 64 + 64]

    def row_view(b, half):
        if half is None:
            return rb.at[b]
        return rb.at[b, half * ROWS : (half + 1) * ROWS]

    own_step = [None] + [zstep(own_view, zos, zor, s) for s in range(1, 5)]
    kv_step = [None] + [zstep(kv_view, zks, zkr, s) for s in range(1, 5)]
    row_step = [None] + [zstep(row_view, rs, rr, s) for s in range(1, 5)]

    def start(pair):
        for q in pair:
            q.start()

    def wait(pair):
        for q in pair:
            q.wait()

    def w1(q):
        own = wb.at[y, q * FFL : (q + 1) * FFL]
        return (
            remote(own, own, ws.at[0, q], wr.at[0, q], ctx(y + 1, z)),
            remote(own, own, ws.at[1, q], wr.at[1, q], ctx(y - 1, z)),
        )

    ym = (y + NY - 1) % NY
    yp = (y + 1) % NY
    w2 = (
        remote(wb.at[ym, 0 : 2 * FFL], wb.at[ym, 0 : 2 * FFL], ws.at[0, 4], wr.at[0, 4], ctx(y + 1, z)),
        remote(wb.at[yp, 2 * FFL : 4 * FFL], wb.at[yp, 2 * FFL : 4 * FFL], ws.at[1, 4], wr.at[1, 4], ctx(y - 1, z)),
    )

    idb[pl.ds(c, 1)] = terms_ref[...].reshape(1, 1, TOK)
    vb[pl.ds(y, 1), 0:2, :] = evec_ref[...].reshape(1, 2, FFL)
    l0.wait()
    l1.wait()
    pl.semaphore_wait(bar, NCTX - 1 + NE - 1)
    rim_copy = remote(x_ref.at[TOK - 16 : TOK], rim, ms_, mr_, {"context": (c + 1) % NCTX})
    rim_copy.start()
    vec_y = [remote(vb.at[y], vb.at[y], vs.at[i], vr.at[i], ctx(y + i + 1, z)) for i in range(3)]
    start(own_step[1])
    start(vec_y)
    kv_y = [remote(kb.at[z, 0], kb.at[z, 3 - i], ks.at[i], kr.at[i], ctx(y + i + 1, z)) for i in range(3)]
    start(kv_y)

    def ids_copy(i):
        return remote(idb.at[c], idb.at[c], d2s.at[i], d2r.at[i], cpeer(i))

    @pl.loop(1, NCTX)
    def _(i):
        ids_copy(i).start()

    wait(load_w)
    start(w1(0))
    start(w1(1))

    hid = hidden_ref[...].astype(F32)
    mean_square = jnp.mean(hid * hid, axis=-1, keepdims=True)
    normed = (hid * lax.rsqrt(mean_square + norm_eps) * gain_ref[...]).astype(BF16)
    base_s[...] = jnp.broadcast_to(
        jnp.sum(hid * ivec_ref[...], axis=-1, keepdims=True), (TOK, 128)
    )

    live = (c * TOK + iota((1, TOK), 1) < len_ref[e]).astype(F32)
    r0, r1 = routes_ref[0:1, :].astype(F32), routes_ref[1:2, :].astype(F32)
    g0, g1 = gates_ref[0:1, :], gates_ref[1:2, :]
    b_rows = b_ref[...]

    def routing():
        eio = iota((16, TOK), 0).astype(F32)
        m0 = r0 == eio
        m1 = r1 == eio
        chosen = jnp.where(m0 | m1, live, 0.0)
        upper = jnp.where(iota((TOK, TOK), 0) < iota((TOK, TOK), 1), 1.0, 0.0).astype(BF16)
        before = dot(chosen.astype(BF16), upper)
        gates = jnp.where(m0, g0, 0.0) + jnp.where(m1, g1, 0.0)
        return chosen, before, gates

    chosen, before, _ = routing()
    sio = iota((16, TOK), 0)
    pieces = []
    for k in range(16):
        ok = (chosen[k : k + 1, :] == 1.0) & (before[k : k + 1, :] == sio.astype(F32)) & (sio < CAP)
        pieces.append(jnp.where(ok, 1.0, 0.0))
    placed = jnp.concatenate(pieces, axis=0).astype(BF16)
    og[...] = dot(placed, normed).astype(BF16).reshape(NE, 32, D)


    def a2a(i):
        return remote(og.at[(e + i) % NE], ar.at[e], as_.at[i], ar_.at[i], epeer(i))

    @pl.loop(1, NE)
    def _(i):
        a2a(i).start()

    ar[pl.ds(e, 1)] = og[pl.ds(e, 1)]

    wait(own_step[1])
    start(own_step[2])

    for t in range(TOK):
        bexp[t] = jnp.broadcast_to(b_rows[:, t : t + 1], (16, 128))
    cf = c_ref[...]
    c_hi = cf.astype(BF16)
    c_lo = (cf - c_hi.astype(F32)).astype(BF16)
    rep = jnp.where(iota((16, 256), 0) == iota((16, 256), 1) % 16, 1.0, 0.0).astype(BF16)
    keep = (iota((TOK, 256), 1) // 16) == (iota((TOK, 256), 0) % 16)
    t_hi = jnp.where(keep, dot_l(c_hi, rep), 0.0).astype(BF16).reshape(8, 16, 256)
    t_lo = jnp.where(keep, dot_l(c_lo, rep), 0.0).astype(BF16).reshape(8, 16, 256)
    cbd[:, 0:16, :] = t_hi
    cbd[:, 16:32, :] = t_lo

    for g in range(KVH):
        for j in range(GROUPS):
            h = g * GROUPS + j
            qs[g, j * TOK : (j + 1) * TOK, :] = query_ref[:, h * HD : (h + 1) * HD]
    acc[...] = jnp.zeros_like(acc)
    ls[...] = jnp.zeros_like(ls)
    ms[...] = jnp.full_like(ms, NEG)
    ma[...] = jnp.zeros_like(ma)
    macc[...] = jnp.zeros_like(macc)
    zs[...] = jnp.zeros_like(zs)

    @pl.loop(1, NE)
    def _(i):
        a2a(i).wait()

    dst = iota((2 * ROWS, 256), 0)
    src = iota((2 * ROWS, 256), 1)
    dl, di, ds = dst // ROWS, (dst % ROWS) // CAP, dst % CAP
    pick = jnp.where(src == di * 32 + dl * 16 + ds, 1.0, 0.0).astype(BF16)
    rb[pl.ds(z, 1)] = dot(pick, ar[...].reshape(256, D)).astype(BF16).reshape(1, 2 * ROWS, D)
    start(row_step[1])
    wait(kv_y)
    start(kv_step[1])
    rim_copy.wait()

    def first(lo, hi):
        @pl.loop(lo, hi)
        def _(k):
            cols = pl.ds(pl.multiple_of(k * BLK, BLK), BLK)
            edge = jnp.where(c == 0, 0.0, rim[:, cols].astype(F32))
            ext[0:8, :] = edge[8:16, :]
            ext[8 : 8 + TOK, :] = x_ref[:, cols].astype(F32)
            for r in range(0, TOK, 32):
                rows = slice(r, r + 32)
                s = cbias_ref[0:1, cols]
                for j in range(KCONV):
                    s = s + taps_ref[j : j + 1, cols] * ext[r + 5 + j : r + 37 + j, :]
                cv = s / (1.0 + jnp.exp(-s))
                raw = dtraw_ref[rows, cols].astype(F32) + dbias_ref[0:1, cols]
                step = jnp.maximum(raw, 0.0) + jnp.log1p(jnp.exp(-jnp.abs(raw)))
                cvs[rows, cols] = cv
                dts[rows, cols] = step
                us[rows, cols] = step * cv
            a2 = a_ref[:, cols] * (-LOG2E)

            def group(g, carried):
                h, total = carried
                base = pl.multiple_of(g * 16, 16)
                d16 = dts[pl.ds(base, 16), cols]
                u16 = us[pl.ds(base, 16), cols]
                for tt in range(16):
                    b = jnp.concatenate([bexp[base + tt]] * (BLK // 128), axis=1)
                    decay = jnp.exp2(a2 * d16[tt : tt + 1, :])
                    h = decay * h + b * u16[tt : tt + 1, :]
                return h, total + jnp.sum(d16, axis=0, keepdims=True)

            h, total = lax.fori_loop(
                0, TOK // 16, group, (jnp.zeros((NSTATE, BLK), F32), jnp.zeros((1, BLK), F32))
            )
            t0 = total.astype(BF16).astype(F32)
            t1 = (total - t0).astype(BF16).astype(F32)
            which = iota((16, BLK), 0)
            total_rows = jnp.where(which == 0, t0, jnp.where(which == 1, t1, total - t0 - t1))
            for i in range(BLK // 128):
                part = jnp.concatenate(
                    [h[:, 128 * i : 128 * i + 128],
                     total_rows[:, 128 * i : 128 * i + 128]],
                    axis=0,
                )
                pe[pl.ds(k * (BLK // 128) + i, 1)] = part.astype(BF16).reshape(1, 32, 128)

    first(0, NBLK // 2)
    wait(own_step[2])
    start(own_step[3])
    first(NBLK // 2, NBLK)

    def end_copy(i):
        return remote(pe.at[(c + i) % NCTX], pr.at[c], ps.at[i], prs.at[i], cpeer(i))

    @pl.loop(1, NCTX)
    def _(i):
        end_copy(i).start()

    pr[pl.ds(c, 1)] = pe[pl.ds(c, 1)]

    start(w1(2))

    def attend(zz):
        key_pos = (((iota((TOK, 512), 1) // TOK + y) % NY) * NZ + zz) * TOK + iota((TOK, 512), 1) % TOK
        allowed = key_pos <= c * TOK + iota((TOK, 512), 0)
        bias = jnp.where(allowed, 0.0, NEG)

        @pl.loop(0, KVH)
        def _(g):
            kcol = pl.ds(pl.multiple_of(g * HD, HD), HD)
            vcol = pl.ds(pl.multiple_of(512 + g * HD, HD), HD)
            kk = kb[pl.ds(zz, 1), :, :, kcol].reshape(NY * TOK, HD)
            vv = kb[pl.ds(zz, 1), :, :, vcol].reshape(NY * TOK, HD)
            scores = dot_t(qs[g], kk)
            scores = (scores.reshape(GROUPS, TOK, 512) + bias[None]).reshape(GROUPS * TOK, 512)
            m_old = ms[g]
            m_new = jnp.maximum(m_old, jnp.max(scores, axis=-1, keepdims=True))
            scale = HD ** (-0.5) * LOG2E
            p = jnp.exp2((scores - jnp.concatenate([m_new] * 4, axis=1)) * scale)
            alpha = jnp.exp2((m_old - m_new) * scale)
            ls[g] = alpha * ls[g] + jnp.sum(p, axis=-1, keepdims=True)
            acc[g] = alpha * acc[g] + dot(p.astype(BF16), vv)
            ms[g] = m_new

    wait(row_step[1])
    start(row_step[2])
    attend(z)
    wait(kv_step[1])
    start(kv_step[2])
    wait(own_step[3])
    start(own_step[4])
    attend((z + 1) % NZ)
    attend((z + NZ - 1) % NZ)

    @pl.loop(1, NCTX)
    def _(i):
        end_copy(i).wait()

    a2c = a_ref[:, pl.ds(pl.multiple_of(c * 128, 128), 128)] * (-LOG2E)

    def join(i, state):
        ic[pl.ds(i, 1)] = state.astype(BF16).reshape(1, NSTATE, 128)
        part = pr[i].astype(F32)
        gone = (part[16:17, :] + part[17:18, :]) + part[18:19, :]
        return jnp.exp2(a2c * gone) * state + part[0:16, :]

    lax.fori_loop(0, NCTX, join, jnp.zeros((NSTATE, 128), F32))

    def inc_copy(i):
        return remote(ic.at[(c + i) % NCTX], ir.at[c], qs_.at[i], qr_.at[i], cpeer(i))

    @pl.loop(1, NCTX)
    def _(i):
        inc_copy(i).start()

    ir[pl.ds(c, 1)] = ic[pl.ds(c, 1)]

    start(w1(3))

    @pl.loop(1, NCTX)
    def _(i):
        ids_copy(i).wait()

    @pl.loop(0, NCTX)
    def _(i):
        row = idb[i][0:1, :]
        lot[pl.ds(i, 1)] = (
            jnp.where(jnp.bitwise_and(row, 127) == iota((128, 128), 0), 1.0, 0.0)
            .astype(BF16).reshape(1, 128, 128)
        )

    def second(lo, hi):
        @pl.loop(lo, hi)
        def _(k):
            cols = pl.ds(pl.multiple_of(k * BLK, BLK), BLK)
            a2 = a_ref[:, cols] * (-LOG2E)
            h0 = jnp.concatenate([ir[k * (BLK // 128) + i] for i in range(BLK // 128)], axis=1).astype(F32)

            def group(g, h):
                base = pl.multiple_of(g * 16, 16)
                rows = pl.ds(base, 16)
                d16 = dts[rows, cols]
                u16 = us[rows, cols]
                for tt in range(16):
                    b = jnp.concatenate([bexp[base + tt]] * (BLK // 128), axis=1)
                    decay = jnp.exp2(a2 * d16[tt : tt + 1, :])
                    h = decay * h + b * u16[tt : tt + 1, :]
                    hb[16 * tt : 16 * tt + 16, :] = h.astype(BF16)
                both = dot(cbd[g], hb[...])
                out = both[0:16, :] + both[16:32, :] + skip_ref[0:1, cols] * cvs[rows, cols]
                zg = z_ref[rows, cols].astype(F32)
                out = (out * (zg / (1.0 + jnp.exp(-zg)))).astype(BF16).astype(F32)
                macc[rows, :] += lane_sum(out * mvec_ref[0:1, cols])
                return h

            lax.fori_loop(0, TOK // 16, group, h0)

    def experts(yb):
        for l in range(2):
            rows = rb[:, l * ROWS : (l + 1) * ROWS, :].reshape(NZ * ROWS, D)
            gate = dot_t(rows, wb[pl.ds(yb, 1), 2 * l * FFL : (2 * l + 1) * FFL, :].reshape(FFL, D))
            up = dot_t(rows, wb[pl.ds(yb, 1), (2 * l + 1) * FFL : (2 * l + 2) * FFL, :].reshape(FFL, D))
            inner = ((gate / (1.0 + jnp.exp(-gate))) * up).astype(BF16).astype(F32)
            term = inner * vb[pl.ds(yb, 1)].reshape(8, FFL)[l : l + 1, :]
            ma[l] += jnp.sum(term, axis=1, keepdims=True)

    wait(row_step[2])
    start(row_step[3])
    wait(kv_step[2])
    start(kv_step[3])
    attend((z + 2) % NZ)
    attend((z + NZ - 2) % NZ)
    for q in range(4):
        wait(w1(q))
    start(w2)
    @pl.loop(1, NCTX)
    def _(i):
        inc_copy(i).wait()

    second(0, NBLK // 2)
    wait(row_step[3])
    start(row_step[4])
    second(NBLK // 2, NBLK)
    wait(kv_step[3])
    start(kv_step[4])
    attend((z + 3) % NZ)
    attend((z + NZ - 3) % NZ)
    wait(vec_y)
    wait(row_step[4])

    @pl.loop(0, 3)
    def _(i):
        experts((y + jnp.where(i == 2, NY - 1, i)) % NY)

    wait(own_step[4])
    wait(kv_step[4])
    attend((z + 4) % NZ)
    wait(w2)
    experts((y + 2) % NY)

    for l in range(2):
        col = ma[l][:, 0:1]
        for q in range(NZ):
            zs[q, l : l + 1, :] = to_row(col[q * ROWS : (q + 1) * ROWS, :])

    def z_copy(i):
        return remote(zs.at[(z + i) % NZ], zr.at[z], z2s.at[i], z2r.at[i], ctx(y, z + i))

    @pl.loop(1, NZ)
    def _(i):
        z_copy(i).start()

    zr[pl.ds(z, 1)] = zs[pl.ds(z, 1)]

    @pl.loop(1, NZ)
    def _(i):
        z_copy(i).wait()

    summed = zr[0]
    for q in range(1, NZ):
        summed = summed + zr[q]
    place = iota((16, 128), 0)
    es[...] = jnp.where(place == 2 * e, summed[0:1, :], 0.0) + jnp.where(
        place == 2 * e + 1, summed[1:2, :], 0.0
    )

    def e_copy(i):
        return remote(es, er.at[e], e2s.at[i], e2r.at[i], epeer(i))

    @pl.loop(1, NE)
    def _(i):
        e_copy(i).start()

    er[pl.ds(e, 1)] = es[...].reshape(1, 16, 128)

    attn = jnp.zeros((TOK, 128), F32)
    for g in range(KVH):
        ratio = (acc[g] / ls[g]).astype(BF16).astype(F32)
        for j in range(GROUPS):
            h = g * GROUPS + j
            attn = attn + ratio[j * TOK : (j + 1) * TOK, :] * avec_ref[0:1, h * HD : (h + 1) * HD]
    attn_col = jnp.sum(attn, axis=1, keepdims=True)
    mamba_col = jnp.sum(macc[...], axis=1, keepdims=True)
    own = to_row(base_s[:, 0:1] + attn_col + mamba_col)
    id_row = terms_ref[...].astype(F32)
    id_same = to_col(id_row) == id_row
    chosen, before, gates = routing()

    @pl.loop(1, NE)
    def _(i):
        e_copy(i).wait()

    back = er[0]
    for q in range(1, NE):
        back = back + er[q]
    value = jnp.zeros((16, TOK), F32)
    for s in range(CAP):
        one = jnp.sum(jnp.where(iota((16, 128), 1) == e * CAP + s, back, 0.0), axis=1, keepdims=True)
        value = value + jnp.where((chosen == 1.0) & (before == float(s)), one, 0.0)
    expert = jnp.sum(value * gates, axis=0, keepdims=True)
    impacts = live * jnp.maximum(own + expert, 0.0)
    imp_ref[...] = impacts

    imp_col = to_col(impacts)
    earlier = iota((TOK, TOK), 0) < iota((TOK, TOK), 1)
    beaten = id_same & ((imp_col > impacts) | ((imp_col == impacts) & earlier))
    beaten = jnp.max(jnp.where(beaten, 1.0, 0.0), axis=0, keepdims=True)
    sent = jnp.where(beaten > 0.0, 0.0, impacts)
    imps[pl.ds(c, 1)] = sent.reshape(1, 1, 128)

    def imp_copy(i):
        return remote(imps.at[c], imps.at[c], i2s.at[i], i2r.at[i], cpeer(i))

    @pl.loop(1, NCTX)
    def _(i):
        imp_copy(i).start()

    @pl.loop(1, NCTX)
    def _(i):
        imp_copy(i).wait()

    def pooled(i):
        word = jnp.right_shift(idb[i][0:1, :], 7) - c * 16
        val = jnp.where(word == iota((16, 128), 0), imps[i][0:1, :], 0.0)
        p0 = val.astype(BF16)
        rest = val - p0.astype(F32)
        p1 = rest.astype(BF16)
        p2 = (rest - p1.astype(F32)).astype(BF16)
        got = dot_t(jnp.concatenate([p0, p1, p2], axis=0), lot[i])
        return (got[0:16] + got[16:32]) + got[32:48]

    def pool(i, best):
        quad = [pooled(8 * i + k) for k in range(8)]
        while len(quad) > 1:
            quad = [jnp.maximum(a, b) for a, b in zip(quad[0::2], quad[1::2])]
        return jnp.maximum(best, quad[0])

    best = lax.fori_loop(0, NCTX // 8, pool, jnp.zeros((16, 128), F32))
    for r in range(16):
        term_ref[0:1, 128 * r : 128 * r + 128] = best[r : r + 1, :]


def shards(
    hidden, query, keys, values, x_inner, z_gate, dt_raw, b_proj, c_proj, conv_weight, conv_bias,
    dt_bias, a_rate, skip_gain, mamba_vector, attn_vector, impact_vector, norm_gain, expert_gate,
    expert_up, expert_vector, routes, route_gate, lengths, term_ids,
):
    dma = pltpu.SemaphoreType.DMA
    vmem = pltpu.VMEM
    outs = pl.pallas_call(
        kernel,
        name="layers",
        out_shape=OUT_SHAPE,
        in_specs=[pl.BlockSpec(memory_space=pltpu.VMEM)] * 12
        + [pl.BlockSpec(memory_space=pltpu.SMEM)]
        + [pl.BlockSpec(memory_space=pltpu.VMEM)] * 10
        + [pl.BlockSpec(memory_space=pl.ANY)] * 2,
        out_specs=OUT_SPECS,
        scratch_shapes=[
            vmem((NY, 4 * FFL, D), BF16), vmem((NZ, NY, TOK, 1024), BF16), vmem((NZ, 2 * ROWS, D), BF16),
            vmem((NE, 32, D), BF16), vmem((NE, 32, D), BF16),
            vmem((TOK, INNER), F32), vmem((TOK, INNER), F32), vmem((TOK, INNER), F32),
            vmem((8 + TOK, BLK), F32), vmem((16, INNER), BF16), vmem((TOK, 16, 128), F32),
            vmem((8, 32, 256), BF16), vmem((256, BLK), BF16),
            vmem((NCTX, 32, 128), BF16), vmem((NCTX, 32, 128), BF16),
            vmem((NCTX, 16, 128), BF16), vmem((NCTX, 16, 128), BF16),
            vmem((KVH, GROUPS * TOK, HD), BF16), vmem((KVH, GROUPS * TOK, HD), F32),
            vmem((KVH, GROUPS * TOK, 128), F32), vmem((KVH, GROUPS * TOK, 128), F32),
            vmem((NY, 8, FFL), F32), vmem((2, NZ * ROWS, 128), F32),
            vmem((NZ, 8, 128), F32), vmem((NZ, 8, 128), F32),
            vmem((16, 128), F32), vmem((NE, 16, 128), F32),
            vmem((NCTX, 1, 128), F32), vmem((NCTX, 1, 128), jnp.int32), vmem((NCTX, 128, 128), BF16),
            vmem((TOK, 128), F32), vmem((TOK, 128), F32),
            dma((6,)), dma((2, 5)), dma((2, 5)), dma((3,)), dma((3,)), dma((3,)), dma((3,)),
            dma((2, 4)), dma((2, 4)), dma((2, 4)), dma((2, 4)), dma((2, 4)), dma((2, 4)), dma((NE,)), dma((NE,)), dma, dma,
            dma((NCTX,)), dma((NCTX,)), dma((NCTX,)), dma((NCTX,)),
            dma((NZ,)), dma((NZ,)), dma((NE,)), dma((NE,)), dma((NCTX,)), dma((NCTX,)),
            dma((NCTX,)), dma((NCTX,)),
        ],
        compiler_params=pltpu.CompilerParams(
            collective_id=0, has_side_effects=True, vmem_limit_bytes=VMEM_LIMIT
        ),
    )(
        hidden[0], query[0], keys[0], values[0], x_inner[0], z_gate[0], dt_raw[0], c_proj[0].T, a_rate,
        b_proj[0].T, routes[0].T, route_gate[0].T, lengths, term_ids, conv_weight, conv_bias[None],
        dt_bias[None], skip_gain[None], mamba_vector[None], attn_vector[None], impact_vector[None],
        norm_gain[None], expert_vector, jnp.swapaxes(expert_gate, 1, 2), jnp.swapaxes(expert_up, 1, 2),
    )
    return tuple(outs)


OUT_SHAPE = (jax.ShapeDtypeStruct((1, TOK), F32), jax.ShapeDtypeStruct((1, VOCAB // NCTX), F32))
OUT_SPECS = (pl.BlockSpec(memory_space=pltpu.VMEM),) * 2
VMEM_LIMIT = 63 << 20


def solution(mesh):
    doc = P("expert", "context", None)
    placed = (doc,) * 9 + (P(),) * 9 + (
        P("expert", None, "context"),
        P("expert", None, "context"),
        P("expert", "context"),
        doc,
        doc,
        P(),
        P("expert", "context"),
    )
    return jax.shard_map(
        shards,
        mesh=mesh,
        in_specs=placed,
        out_specs=(P("expert", "context"), P("expert", "context")),
        check_vma=False,
    )
```

```python
import jax
import jax.numpy as jnp
from jax import lax
from jax.experimental import pallas as pl
from jax.experimental.pallas import tpu as pltpu
from jax.sharding import PartitionSpec as P

H = 16
HD = 128
KVH = 4
GROUPS = H // KVH
KCONV = 4
VOCAB = 65536
D = 2048
INNER = 4096
NSTATE = 16
TOK = 128
CAP = 10
NE = 8
NCTX = 32
NY = 4
NZ = 8
FFL = 224
BLK = 512
NBLK = INNER // BLK
ROWS = NE * CAP
LOG2E = 1.4426950408889634
MESH = pl.DeviceIdType.MESH
F32 = jnp.float32
BF16 = jnp.bfloat16

NEG = -1e30
norm_eps = 1e-06


def iota(shape, axis):
    return lax.broadcasted_iota(jnp.int32, shape, axis)


def dot(a, b):
    return lax.dot_general(a, b, (((1,), (0,)), ((), ())), preferred_element_type=F32)


def dot_t(a, b):
    return lax.dot_general(a, b, (((1,), (1,)), ((), ())), preferred_element_type=F32)


def dot_l(a, b):
    return lax.dot_general(a, b, (((0,), (0,)), ((), ())), preferred_element_type=F32)


def remote(src, dst, send, recv, device):
    return pltpu.make_async_remote_copy(
        src_ref=src, dst_ref=dst, send_sem=send, recv_sem=recv,
        device_id=device, device_id_type=MESH,
    )


def lane_sum(x):
    total = x[:, 0:128]
    for i in range(1, x.shape[1] // 128):
        total = total + x[:, 128 * i : 128 * (i + 1)]
    return total


def to_row(col):
    n = col.shape[0]
    eye = iota((n, 128), 0) == iota((n, 128), 1)
    return jnp.sum(jnp.where(eye, col, 0.0), axis=0, keepdims=True)


def to_col(row):
    eye = iota((128, 128), 0) == iota((128, 128), 1)
    return jnp.sum(jnp.where(eye, row, 0.0), axis=1, keepdims=True)


def kernel(
    hidden_ref, query_ref, keys_ref, values_ref, x_ref, z_ref, dtraw_ref, c_ref, a_ref,
    b_ref, routes_ref, gates_ref, len_ref, terms_ref, taps_ref, cbias_ref, dbias_ref, skip_ref, mvec_ref,
    avec_ref, ivec_ref, gain_ref, evec_ref, gate_ref, up_ref,
    imp_ref, term_ref,
    wb, kb, rb, og, ar, dts, us, cvs, ext, rim, bexp, cbd, hb, pe, pr, ic, ir,
    qs, acc, ms, ls, vb, ma, zs, zr, es, er, imps, idb, lot, macc, base_s,
    lsem, ws, wr, ks, kr, vs, vr, zos, zor, zks, zkr, rs, rr, as_, ar_, ms_, mr_, ps, prs, qs_, qr_,
    z2s, z2r, e2s, e2r, i2s, i2r, d2s, d2r,
):
    e = lax.axis_index("expert")
    c = lax.axis_index("context")
    y = c // NZ
    z = c % NZ

    def ctx(yy, zz):
        return {"context": ((yy + NY) % NY) * NZ + (zz + NZ) % NZ}

    def cpeer(i):
        return {"context": (c + i) % NCTX}

    def epeer(i):
        return {"expert": (e + i) % NE}

    bar = pltpu.get_barrier_semaphore()

    @pl.loop(1, NCTX)
    def _(i):
        pl.semaphore_signal(bar, inc=1, device_id=cpeer(i), device_id_type=MESH)

    @pl.loop(1, NE)
    def _(i):
        pl.semaphore_signal(bar, inc=1, device_id=epeer(i), device_id_type=MESH)

    l0 = pltpu.make_async_copy(keys_ref, kb.at[z, 0, :, 0:512], lsem.at[0])
    l1 = pltpu.make_async_copy(values_ref, kb.at[z, 0, :, 512:1024], lsem.at[1])
    load_w = []
    for l in range(2):
        at = 2 * FFL * l
        load_w.append(pltpu.make_async_copy(gate_ref.at[l], wb.at[y, at : at + FFL], lsem.at[2 + 2 * l]))
        at = at + FFL
        load_w.append(pltpu.make_async_copy(up_ref.at[l], wb.at[y, at : at + FFL], lsem.at[3 + 2 * l]))
    l0.start()
    l1.start()
    for k in load_w:
        k.start()

    def zstep(view, ss, rr_, s):
        bp = (z - (s - 1) + NZ) % NZ
        bm = (z + (s - 1)) % NZ
        p, m = view(bp, 0 if s == 4 else None), view(bm, 1 if s == 4 else None)
        return (
            remote(p, p, ss.at[0, s - 1], rr_.at[0, s - 1], ctx(y, z + 1)),
            remote(m, m, ss.at[1, s - 1], rr_.at[1, s - 1], ctx(y, z - 1)),
        )

    def own_view(b, half):
        if half is None:
            return kb.at[b, 0]
        return kb.at[b, 0, half * 64 : half * 64 + 64]

    def kv_view(b, half):
        if half is None:
            return kb.at[b, 1:NY]
        return kb.at[b, 1:NY, half * 64 : half * 64 + 64]

    def row_view(b, half):
        if half is None:
            return rb.at[b]
        return rb.at[b, half * ROWS : (half + 1) * ROWS]

    own_step = [None] + [zstep(own_view, zos, zor, s) for s in range(1, 5)]
    kv_step = [None] + [zstep(kv_view, zks, zkr, s) for s in range(1, 5)]
    row_step = [None] + [zstep(row_view, rs, rr, s) for s in range(1, 5)]

    def start(pair):
        for q in pair:
            q.start()

    def wait(pair):
        for q in pair:
            q.wait()

    def w1(q):
        own = wb.at[y, q * FFL : (q + 1) * FFL]
        return (
            remote(own, own, ws.at[0, q], wr.at[0, q], ctx(y + 1, z)),
            remote(own, own, ws.at[1, q], wr.at[1, q], ctx(y - 1, z)),
        )

    ym = (y + NY - 1) % NY
    yp = (y + 1) % NY
    w2 = (
        remote(wb.at[ym, 0 : 2 * FFL], wb.at[ym, 0 : 2 * FFL], ws.at[0, 4], wr.at[0, 4], ctx(y + 1, z)),
        remote(wb.at[yp, 2 * FFL : 4 * FFL], wb.at[yp, 2 * FFL : 4 * FFL], ws.at[1, 4], wr.at[1, 4], ctx(y - 1, z)),
    )

    idb[pl.ds(c, 1)] = terms_ref[...].reshape(1, 1, TOK)
    vb[pl.ds(y, 1), 0:2, :] = evec_ref[...].reshape(1, 2, FFL)
    l0.wait()
    l1.wait()
    pl.semaphore_wait(bar, NCTX - 1 + NE - 1)
    rim_copy = remote(x_ref.at[TOK - 16 : TOK], rim, ms_, mr_, {"context": (c + 1) % NCTX})
    rim_copy.start()
    vec_y = [remote(vb.at[y], vb.at[y], vs.at[i], vr.at[i], ctx(y + i + 1, z)) for i in range(3)]
    start(own_step[1])
    start(vec_y)
    kv_y = [remote(kb.at[z, 0], kb.at[z, 3 - i], ks.at[i], kr.at[i], ctx(y + i + 1, z)) for i in range(3)]
    start(kv_y)

    def ids_copy(i):
        return remote(idb.at[c], idb.at[c], d2s.at[i], d2r.at[i], cpeer(i))

    @pl.loop(1, NCTX)
    def _(i):
        ids_copy(i).start()

    wait(load_w)
    start(w1(0))
    start(w1(1))

    hid = hidden_ref[...].astype(F32)
    mean_square = jnp.mean(hid * hid, axis=-1, keepdims=True)
    normed = (hid * lax.rsqrt(mean_square + norm_eps) * gain_ref[...]).astype(BF16)
    base_s[...] = jnp.broadcast_to(
        jnp.sum(hid * ivec_ref[...], axis=-1, keepdims=True), (TOK, 128)
    )

    live = (c * TOK + iota((1, TOK), 1) < len_ref[e]).astype(F32)
    r0, r1 = routes_ref[0:1, :].astype(F32), routes_ref[1:2, :].astype(F32)
    g0, g1 = gates_ref[0:1, :], gates_ref[1:2, :]
    b_rows = b_ref[...]

    def routing():
        eio = iota((16, TOK), 0).astype(F32)
        m0 = r0 == eio
        m1 = r1 == eio
        chosen = jnp.where(m0 | m1, live, 0.0)
        upper = jnp.where(iota((TOK, TOK), 0) < iota((TOK, TOK), 1), 1.0, 0.0).astype(BF16)
        before = dot(chosen.astype(BF16), upper)
        gates = jnp.where(m0, g0, 0.0) + jnp.where(m1, g1, 0.0)
        return chosen, before, gates

    chosen, before, _ = routing()
    sio = iota((16, TOK), 0)
    pieces = []
    for k in range(16):
        ok = (chosen[k : k + 1, :] == 1.0) & (before[k : k + 1, :] == sio.astype(F32)) & (sio < CAP)
        pieces.append(jnp.where(ok, 1.0, 0.0))
    placed = jnp.concatenate(pieces, axis=0).astype(BF16)
    og[...] = dot(placed, normed).astype(BF16).reshape(NE, 32, D)


    def a2a(i):
        return remote(og.at[(e + i) % NE], ar.at[e], as_.at[i], ar_.at[i], epeer(i))

    @pl.loop(1, NE)
    def _(i):
        a2a(i).start()

    ar[pl.ds(e, 1)] = og[pl.ds(e, 1)]

    wait(own_step[1])
    start(own_step[2])

    for t in range(TOK):
        bexp[t] = jnp.broadcast_to(b_rows[:, t : t + 1], (16, 128))
    cf = c_ref[...]
    c_hi = cf.astype(BF16)
    c_lo = (cf - c_hi.astype(F32)).astype(BF16)
    rep = jnp.where(iota((16, 256), 0) == iota((16, 256), 1) % 16, 1.0, 0.0).astype(BF16)
    keep = (iota((TOK, 256), 1) // 16) == (iota((TOK, 256), 0) % 16)
    t_hi = jnp.where(keep, dot_l(c_hi, rep), 0.0).astype(BF16).reshape(8, 16, 256)
    t_lo = jnp.where(keep, dot_l(c_lo, rep), 0.0).astype(BF16).reshape(8, 16, 256)
    cbd[:, 0:16, :] = t_hi
    cbd[:, 16:32, :] = t_lo

    for g in range(KVH):
        for j in range(GROUPS):
            h = g * GROUPS + j
            qs[g, j * TOK : (j + 1) * TOK, :] = query_ref[:, h * HD : (h + 1) * HD]
    acc[...] = jnp.zeros_like(acc)
    ls[...] = jnp.zeros_like(ls)
    ms[...] = jnp.full_like(ms, NEG)
    ma[...] = jnp.zeros_like(ma)
    macc[...] = jnp.zeros_like(macc)
    zs[...] = jnp.zeros_like(zs)

    @pl.loop(1, NE)
    def _(i):
        a2a(i).wait()

    dst = iota((2 * ROWS, 256), 0)
    src = iota((2 * ROWS, 256), 1)
    dl, di, ds = dst // ROWS, (dst % ROWS) // CAP, dst % CAP
    pick = jnp.where(src == di * 32 + dl * 16 + ds, 1.0, 0.0).astype(BF16)
    rb[pl.ds(z, 1)] = dot(pick, ar[...].reshape(256, D)).astype(BF16).reshape(1, 2 * ROWS, D)
    start(row_step[1])
    wait(kv_y)
    start(kv_step[1])
    rim_copy.wait()

    def first(lo, hi):
        @pl.loop(lo, hi)
        def _(k):
            cols = pl.ds(pl.multiple_of(k * BLK, BLK), BLK)
            edge = jnp.where(c == 0, 0.0, rim[:, cols].astype(F32))
            ext[0:8, :] = edge[8:16, :]
            ext[8 : 8 + TOK, :] = x_ref[:, cols].astype(F32)
            for r in range(0, TOK, 32):
                rows = slice(r, r + 32)
                s = cbias_ref[0:1, cols]
                for j in range(KCONV):
                    s = s + taps_ref[j : j + 1, cols] * ext[r + 5 + j : r + 37 + j, :]
                cv = s / (1.0 + jnp.exp(-s))
                raw = dtraw_ref[rows, cols].astype(F32) + dbias_ref[0:1, cols]
                step = jnp.maximum(raw, 0.0) + jnp.log1p(jnp.exp(-jnp.abs(raw)))
                cvs[rows, cols] = cv
                dts[rows, cols] = step
                us[rows, cols] = step * cv
            a2 = a_ref[:, cols] * (-LOG2E)

            def group(g, carried):
                h, total = carried
                base = pl.multiple_of(g * 16, 16)
                d16 = dts[pl.ds(base, 16), cols]
                u16 = us[pl.ds(base, 16), cols]
                for tt in range(16):
                    b = jnp.concatenate([bexp[base + tt]] * (BLK // 128), axis=1)
                    decay = jnp.exp2(a2 * d16[tt : tt + 1, :])
                    h = decay * h + b * u16[tt : tt + 1, :]
                return h, total + jnp.sum(d16, axis=0, keepdims=True)

            h, total = lax.fori_loop(
                0, TOK // 16, group, (jnp.zeros((NSTATE, BLK), F32), jnp.zeros((1, BLK), F32))
            )
            t0 = total.astype(BF16).astype(F32)
            t1 = (total - t0).astype(BF16).astype(F32)
            which = iota((16, BLK), 0)
            total_rows = jnp.where(which == 0, t0, jnp.where(which == 1, t1, total - t0 - t1))
            for i in range(BLK // 128):
                part = jnp.concatenate(
                    [h[:, 128 * i : 128 * i + 128],
                     total_rows[:, 128 * i : 128 * i + 128]],
                    axis=0,
                )
                pe[pl.ds(k * (BLK // 128) + i, 1)] = part.astype(BF16).reshape(1, 32, 128)

    first(0, NBLK // 2)
    wait(own_step[2])
    start(own_step[3])
    first(NBLK // 2, NBLK)

    def end_copy(i):
        return remote(pe.at[(c + i) % NCTX], pr.at[c], ps.at[i], prs.at[i], cpeer(i))

    @pl.loop(1, NCTX)
    def _(i):
        end_copy(i).start()

    pr[pl.ds(c, 1)] = pe[pl.ds(c, 1)]

    start(w1(2))

    def attend(zz):
        key_pos = (((iota((TOK, 512), 1) // TOK + y) % NY) * NZ + zz) * TOK + iota((TOK, 512), 1) % TOK
        allowed = key_pos <= c * TOK + iota((TOK, 512), 0)
        bias = jnp.where(allowed, 0.0, NEG)

        @pl.loop(0, KVH)
        def _(g):
            kcol = pl.ds(pl.multiple_of(g * HD, HD), HD)
            vcol = pl.ds(pl.multiple_of(512 + g * HD, HD), HD)
            kk = kb[pl.ds(zz, 1), :, :, kcol].reshape(NY * TOK, HD)
            vv = kb[pl.ds(zz, 1), :, :, vcol].reshape(NY * TOK, HD)
            scores = dot_t(qs[g], kk)
            scores = (scores.reshape(GROUPS, TOK, 512) + bias[None]).reshape(GROUPS * TOK, 512)
            m_old = ms[g]
            m_new = jnp.maximum(m_old, jnp.max(scores, axis=-1, keepdims=True))
            scale = HD ** (-0.5) * LOG2E
            p = jnp.exp2((scores - jnp.concatenate([m_new] * 4, axis=1)) * scale)
            alpha = jnp.exp2((m_old - m_new) * scale)
            ls[g] = alpha * ls[g] + jnp.sum(p, axis=-1, keepdims=True)
            acc[g] = alpha * acc[g] + dot(p.astype(BF16), vv)
            ms[g] = m_new

    wait(row_step[1])
    start(row_step[2])
    attend(z)
    wait(kv_step[1])
    start(kv_step[2])
    wait(own_step[3])
    start(own_step[4])
    attend((z + 1) % NZ)
    attend((z + NZ - 1) % NZ)

    @pl.loop(1, NCTX)
    def _(i):
        end_copy(i).wait()

    a2c = a_ref[:, pl.ds(pl.multiple_of(c * 128, 128), 128)] * (-LOG2E)

    def join(i, state):
        ic[pl.ds(i, 1)] = state.astype(BF16).reshape(1, NSTATE, 128)
        part = pr[i].astype(F32)
        gone = (part[16:17, :] + part[17:18, :]) + part[18:19, :]
        return jnp.exp2(a2c * gone) * state + part[0:16, :]

    lax.fori_loop(0, NCTX, join, jnp.zeros((NSTATE, 128), F32))

    def inc_copy(i):
        return remote(ic.at[(c + i) % NCTX], ir.at[c], qs_.at[i], qr_.at[i], cpeer(i))

    @pl.loop(1, NCTX)
    def _(i):
        inc_copy(i).start()

    ir[pl.ds(c, 1)] = ic[pl.ds(c, 1)]

    start(w1(3))

    @pl.loop(1, NCTX)
    def _(i):
        ids_copy(i).wait()

    @pl.loop(0, NCTX)
    def _(i):
        row = idb[i][0:1, :]
        lot[pl.ds(i, 1)] = (
            jnp.where(jnp.bitwise_and(row, 127) == iota((128, 128), 0), 1.0, 0.0)
            .astype(BF16).reshape(1, 128, 128)
        )

    def second(lo, hi):
        @pl.loop(lo, hi)
        def _(k):
            cols = pl.ds(pl.multiple_of(k * BLK, BLK), BLK)
            a2 = a_ref[:, cols] * (-LOG2E)
            h0 = jnp.concatenate([ir[k * (BLK // 128) + i] for i in range(BLK // 128)], axis=1).astype(F32)

            def group(g, h):
                base = pl.multiple_of(g * 16, 16)
                rows = pl.ds(base, 16)
                d16 = dts[rows, cols]
                u16 = us[rows, cols]
                for tt in range(16):
                    b = jnp.concatenate([bexp[base + tt]] * (BLK // 128), axis=1)
                    decay = jnp.exp2(a2 * d16[tt : tt + 1, :])
                    h = decay * h + b * u16[tt : tt + 1, :]
                    hb[16 * tt : 16 * tt + 16, :] = h.astype(BF16)
                both = dot(cbd[g], hb[...])
                out = both[0:16, :] + both[16:32, :] + skip_ref[0:1, cols] * cvs[rows, cols]
                zg = z_ref[rows, cols].astype(F32)
                out = (out * (zg / (1.0 + jnp.exp(-zg)))).astype(BF16).astype(F32)
                macc[rows, :] += lane_sum(out * mvec_ref[0:1, cols])
                return h

            lax.fori_loop(0, TOK // 16, group, h0)

    def experts(yb):
        for l in range(2):
            rows = rb[:, l * ROWS : (l + 1) * ROWS, :].reshape(NZ * ROWS, D)
            gate = dot_t(rows, wb[pl.ds(yb, 1), 2 * l * FFL : (2 * l + 1) * FFL, :].reshape(FFL, D))
            up = dot_t(rows, wb[pl.ds(yb, 1), (2 * l + 1) * FFL : (2 * l + 2) * FFL, :].reshape(FFL, D))
            inner = ((gate / (1.0 + jnp.exp(-gate))) * up).astype(BF16).astype(F32)
            term = inner * vb[pl.ds(yb, 1)].reshape(8, FFL)[l : l + 1, :]
            ma[l] += jnp.sum(term, axis=1, keepdims=True)

    wait(row_step[2])
    start(row_step[3])
    wait(kv_step[2])
    start(kv_step[3])
    attend((z + 2) % NZ)
    attend((z + NZ - 2) % NZ)
    for q in range(4):
        wait(w1(q))
    start(w2)
    @pl.loop(1, NCTX)
    def _(i):
        inc_copy(i).wait()

    second(0, NBLK // 2)
    wait(row_step[3])
    start(row_step[4])
    second(NBLK // 2, NBLK)
    wait(kv_step[3])
    start(kv_step[4])
    attend((z + 3) % NZ)
    attend((z + NZ - 3) % NZ)
    wait(vec_y)
    wait(row_step[4])

    @pl.loop(0, 3)
    def _(i):
        experts((y + jnp.where(i == 2, NY - 1, i)) % NY)

    wait(w2)
    experts((y + 2) % NY)

    for l in range(2):
        col = ma[l][:, 0:1]
        for q in range(NZ):
            zs[q, l : l + 1, :] = to_row(col[q * ROWS : (q + 1) * ROWS, :])

    def z_copy(i):
        return remote(zs.at[(z + i) % NZ], zr.at[z], z2s.at[i], z2r.at[i], ctx(y, z + i))

    @pl.loop(1, NZ)
    def _(i):
        z_copy(i).start()

    zr[pl.ds(z, 1)] = zs[pl.ds(z, 1)]
    wait(own_step[4])
    wait(kv_step[4])
    attend((z + 4) % NZ)

    @pl.loop(1, NZ)
    def _(i):
        z_copy(i).wait()

    summed = zr[0]
    for q in range(1, NZ):
        summed = summed + zr[q]
    place = iota((16, 128), 0)
    es[...] = jnp.where(place == 2 * e, summed[0:1, :], 0.0) + jnp.where(
        place == 2 * e + 1, summed[1:2, :], 0.0
    )

    def e_copy(i):
        return remote(es, er.at[e], e2s.at[i], e2r.at[i], epeer(i))

    @pl.loop(1, NE)
    def _(i):
        e_copy(i).start()

    er[pl.ds(e, 1)] = es[...].reshape(1, 16, 128)

    attn = jnp.zeros((TOK, 128), F32)
    for g in range(KVH):
        ratio = (acc[g] / ls[g]).astype(BF16).astype(F32)
        for j in range(GROUPS):
            h = g * GROUPS + j
            attn = attn + ratio[j * TOK : (j + 1) * TOK, :] * avec_ref[0:1, h * HD : (h + 1) * HD]
    attn_col = jnp.sum(attn, axis=1, keepdims=True)
    mamba_col = jnp.sum(macc[...], axis=1, keepdims=True)
    own = to_row(base_s[:, 0:1] + attn_col + mamba_col)
    id_row = terms_ref[...].astype(F32)
    id_same = to_col(id_row) == id_row
    chosen, before, gates = routing()

    @pl.loop(1, NE)
    def _(i):
        e_copy(i).wait()

    back = er[0]
    for q in range(1, NE):
        back = back + er[q]
    value = jnp.zeros((16, TOK), F32)
    for s in range(CAP):
        one = jnp.sum(jnp.where(iota((16, 128), 1) == e * CAP + s, back, 0.0), axis=1, keepdims=True)
        value = value + jnp.where((chosen == 1.0) & (before == float(s)), one, 0.0)
    expert = jnp.sum(value * gates, axis=0, keepdims=True)
    impacts = live * jnp.maximum(own + expert, 0.0)
    imp_ref[...] = impacts

    imp_col = to_col(impacts)
    earlier = iota((TOK, TOK), 0) < iota((TOK, TOK), 1)
    beaten = id_same & ((imp_col > impacts) | ((imp_col == impacts) & earlier))
    beaten = jnp.max(jnp.where(beaten, 1.0, 0.0), axis=0, keepdims=True)
    sent = jnp.where(beaten > 0.0, 0.0, impacts)
    imps[pl.ds(c, 1)] = sent.reshape(1, 1, 128)

    def imp_copy(i):
        return remote(imps.at[c], imps.at[c], i2s.at[i], i2r.at[i], cpeer(i))

    @pl.loop(1, NCTX)
    def _(i):
        imp_copy(i).start()

    @pl.loop(1, NCTX)
    def _(i):
        imp_copy(i).wait()

    def pooled(i):
        word = jnp.right_shift(idb[i][0:1, :], 7) - c * 16
        val = jnp.where(word == iota((16, 128), 0), imps[i][0:1, :], 0.0)
        p0 = val.astype(BF16)
        rest = val - p0.astype(F32)
        p1 = rest.astype(BF16)
        p2 = (rest - p1.astype(F32)).astype(BF16)
        got = dot_t(jnp.concatenate([p0, p1, p2], axis=0), lot[i])
        return (got[0:16] + got[16:32]) + got[32:48]

    def pool(i, best):
        quad = [pooled(8 * i + k) for k in range(8)]
        while len(quad) > 1:
            quad = [jnp.maximum(a, b) for a, b in zip(quad[0::2], quad[1::2])]
        return jnp.maximum(best, quad[0])

    best = lax.fori_loop(0, NCTX // 8, pool, jnp.zeros((16, 128), F32))
    for r in range(16):
        term_ref[0:1, 128 * r : 128 * r + 128] = best[r : r + 1, :]


def shards(
    hidden, query, keys, values, x_inner, z_gate, dt_raw, b_proj, c_proj, conv_weight, conv_bias,
    dt_bias, a_rate, skip_gain, mamba_vector, attn_vector, impact_vector, norm_gain, expert_gate,
    expert_up, expert_vector, routes, route_gate, lengths, term_ids,
):
    dma = pltpu.SemaphoreType.DMA
    vmem = pltpu.VMEM
    outs = pl.pallas_call(
        kernel,
        name="layers",
        out_shape=OUT_SHAPE,
        in_specs=[pl.BlockSpec(memory_space=pltpu.VMEM)] * 12
        + [pl.BlockSpec(memory_space=pltpu.SMEM)]
        + [pl.BlockSpec(memory_space=pltpu.VMEM)] * 10
        + [pl.BlockSpec(memory_space=pl.ANY)] * 2,
        out_specs=OUT_SPECS,
        scratch_shapes=[
            vmem((NY, 4 * FFL, D), BF16), vmem((NZ, NY, TOK, 1024), BF16), vmem((NZ, 2 * ROWS, D), BF16),
            vmem((NE, 32, D), BF16), vmem((NE, 32, D), BF16),
            vmem((TOK, INNER), F32), vmem((TOK, INNER), F32), vmem((TOK, INNER), F32),
            vmem((8 + TOK, BLK), F32), vmem((16, INNER), BF16), vmem((TOK, 16, 128), F32),
            vmem((8, 32, 256), BF16), vmem((256, BLK), BF16),
            vmem((NCTX, 32, 128), BF16), vmem((NCTX, 32, 128), BF16),
            vmem((NCTX, 16, 128), BF16), vmem((NCTX, 16, 128), BF16),
            vmem((KVH, GROUPS * TOK, HD), BF16), vmem((KVH, GROUPS * TOK, HD), F32),
            vmem((KVH, GROUPS * TOK, 128), F32), vmem((KVH, GROUPS * TOK, 128), F32),
            vmem((NY, 8, FFL), F32), vmem((2, NZ * ROWS, 128), F32),
            vmem((NZ, 8, 128), F32), vmem((NZ, 8, 128), F32),
            vmem((16, 128), F32), vmem((NE, 16, 128), F32),
            vmem((NCTX, 1, 128), F32), vmem((NCTX, 1, 128), jnp.int32), vmem((NCTX, 128, 128), BF16),
            vmem((TOK, 128), F32), vmem((TOK, 128), F32),
            dma((6,)), dma((2, 5)), dma((2, 5)), dma((3,)), dma((3,)), dma((3,)), dma((3,)),
            dma((2, 4)), dma((2, 4)), dma((2, 4)), dma((2, 4)), dma((2, 4)), dma((2, 4)), dma((NE,)), dma((NE,)), dma, dma,
            dma((NCTX,)), dma((NCTX,)), dma((NCTX,)), dma((NCTX,)),
            dma((NZ,)), dma((NZ,)), dma((NE,)), dma((NE,)), dma((NCTX,)), dma((NCTX,)),
            dma((NCTX,)), dma((NCTX,)),
        ],
        compiler_params=pltpu.CompilerParams(
            collective_id=0, has_side_effects=True, vmem_limit_bytes=VMEM_LIMIT
        ),
    )(
        hidden[0], query[0], keys[0], values[0], x_inner[0], z_gate[0], dt_raw[0], c_proj[0].T, a_rate,
        b_proj[0].T, routes[0].T, route_gate[0].T, lengths, term_ids, conv_weight, conv_bias[None],
        dt_bias[None], skip_gain[None], mamba_vector[None], attn_vector[None], impact_vector[None],
        norm_gain[None], expert_vector, jnp.swapaxes(expert_gate, 1, 2), jnp.swapaxes(expert_up, 1, 2),
    )
    return tuple(outs)


OUT_SHAPE = (jax.ShapeDtypeStruct((1, TOK), F32), jax.ShapeDtypeStruct((1, VOCAB // NCTX), F32))
OUT_SPECS = (pl.BlockSpec(memory_space=pltpu.VMEM),) * 2
VMEM_LIMIT = 63 << 20


def solution(mesh):
    doc = P("expert", "context", None)
    placed = (doc,) * 9 + (P(),) * 9 + (
        P("expert", None, "context"),
        P("expert", None, "context"),
        P("expert", "context"),
        doc,
        doc,
        P(),
        P("expert", "context"),
    )
    return jax.shard_map(
        shards,
        mesh=mesh,
        in_specs=placed,
        out_specs=(P("expert", "context"), P("expert", "context")),
        check_vma=False,
    )
```
